32 devices in a mesh: group: 4 (over y, core), tile: 8 (over z, x).
Axes of the slice: x: 2, y: 2, z: 4, core: 2. Of those that a mesh axis runs over, the one named last changes fastest.
Arguments:
- features: bfloat16 [65536, 128], P(('group', 'tile')), may hold values from -6 to 6
- kernel_map: int32 [32, 27, 2048], P(('group', 'tile')), may hold values from 0 to 2560, as said below
- send_order: int32 [32, 2048], P(('group', 'tile')), may hold values from 0 to 2047, each once within a row
- counts: int32 [32], P(('group', 'tile')), may hold values from 1 to 2048, 49152 in all
- first_weight: bfloat16 [27, 128, 128], replicated, may hold values from -0.109375 to 0.109375
- second_weight: bfloat16 [27, 128, 128], replicated, may hold values from -0.109375 to 0.109375
- norm_gain: float32 [128], replicated, may hold values from 0.1 to 1.9
- cotangent: bfloat16 [65536, 128], P(('group', 'tile')), may hold values from -6 to 6
Outputs:
- serial_out: bfloat16 [65536, 128], P(('group', 'tile'))
- grad_features: bfloat16 [65536, 128], P(('group', 'tile'))
- first_grad: float32 [27, 128, 128], replicated
- second_grad: float32 [27, 128, 128], replicated
- gain_grad: float32 [128], replicated
The draws below stay inside these ranges and needn't reach their ends.
Inputs may be any that keep to these rules, and one draw needn't show every extreme that they name: `kernel_map`: entry [d, k, i] is the row of tile d's table read by voxel slot i for offset k: rows 0 to 255 are the previous tile's slots 256 to 511, then the tile's own 2048 slots, then the next tile's first 256 slots, and 2560 means no neighbour. Offset 13 is the voxel itself. Only slots below 256 read the previous tile, only slots 256 to 511 read the next. `send_order`: each row holds every slot once. `counts`: the largest is exactly 2048.
All inputs are finite; a program needn't handle non-finite values. No bound on the sum of `counts` on one device may be relied on, other than what follows from the above.
Results may differ from the reference program's by a relative error of at most 0.0049.
Values may be sent and summed in bfloat16 or wider, within the bound.
No kernel may reach another device: no remote copies, remote signals or barrier semaphores. Data moves between devices by JAX's collectives and lax.ppermute only.
A program may use at most 192 MiB of HBM per device.

```python
import math
import jax
import jax.numpy as jnp
import numpy as np
from jax import lax

C = 128
KVOL = 27
V = 2048
F = 256
N = 65536
N_GROUP = 4
N_TILE = 8


def draw_kernel_map(key, part):
    tiles = N_GROUP * N_TILE
    key_cat, key_local, key_face = jax.random.split(jax.random.fold_in(key, 17), 3)
    shape = (tiles, KVOL, V)
    category = jax.random.randint(key_cat, shape, 0, 10)
    local_rows = jax.random.randint(key_local, shape, F, V + F)
    face_rows = jax.random.randint(key_face, shape, 0, F)
    slot = jnp.arange(V, dtype=jnp.int32)[None, None, :]
    low_slot = slot < F
    high_slot = (slot >= F) & (slot < 2 * F)
    remote = (category >= 2) & (category < 5)
    chosen = jnp.where(category < 2, V + 2 * F, local_rows)
    chosen = jnp.where(remote & low_slot, face_rows, chosen)
    chosen = jnp.where(remote & high_slot, V + F + face_rows, chosen)
    offset = jnp.arange(KVOL, dtype=jnp.int32)[None, :, None]
    chosen = jnp.where(offset == 13, F + slot, chosen)
    return chosen.astype(jnp.int32)


def block_levels(own_key, dims, cuts, low, top_value):
    def one(dim, parts):
        heights = jax.random.uniform(jax.random.fold_in(jax.random.fold_in(own_key, 6), dim), (parts,), jnp.float32, low / len(cuts), top_value / len(cuts))
        return jnp.repeat(jnp.exp(heights), dims[dim] // parts).reshape((-1,) + (1,) * (len(dims) - dim - 1))

    level = one(*cuts[0])
    for cut in cuts[1:]:
        level = level * one(*cut)
    return level


def profile(count, total, bound, slope):
    weights = [(1 << 20) // math.isqrt(rank ** slope) + 1 for rank in range(2, count + 1)]
    spare, given = total - bound - (count - 1), [1] * (count - 1)
    while spare > 0:
        movable = [i for i in range(count - 1) if given[i] < bound]
        mass, remaining = sum([weights[i] for i in movable]), spare
        for i in movable:
            more = min(bound - given[i], max(1, remaining * weights[i] // mass), spare)
            given[i] = given[i] + more
            spare = spare - more
    return np.array([bound] + given)


def ragged(own_key, count, total, reach, skew):
    if count == 2:
        one = jax.random.randint(own_key, (), max(1, total - reach), min(reach, total - 1) + 1)
        return jnp.stack([one, total - one])
    sizes = jnp.asarray(profile(count, total, reach, skew), jnp.int32)
    couples = (count - 1) // 2
    donor, receiver = sizes[1:1 + 2 * couples:2], sizes[2:2 + 2 * couples:2]
    margin = jnp.minimum(donor - 1, reach - receiver)
    shifted = jax.random.randint(jax.random.fold_in(own_key, 1), (couples,), 0, 1 << 20) % (margin + 1)
    sizes = sizes.at[1:1 + 2 * couples:2].set(donor - shifted).at[2:2 + 2 * couples:2].set(receiver + shifted)
    return sizes[jax.random.permutation(jax.random.fold_in(own_key, 2), count)]


def noise(key, dims, scale, bound, cuts=(), kind=jnp.bfloat16):
    drawn = scale * jax.random.normal(key, dims, jnp.float32)
    if cuts:
        drawn = drawn * block_levels(key, dims, cuts, -0.22, 0.18)
    return jnp.clip(drawn, -bound, bound).astype(kind)


def setup_inputs(seed: int = 0) -> dict:
    key_list = jax.random.split(jax.random.key(seed), 9)
    return {
        "features": noise(key_list[0], (N, C), 1.0, 6.0, ((0, 32),)),
        "kernel_map": draw_kernel_map(jax.random.fold_in(key_list[8], 71), 0),
        "send_order": jax.vmap(lambda own: jax.random.permutation(own, V))(jax.random.split(key_list[2], (N_GROUP * N_TILE))).reshape((N_GROUP * N_TILE, V)).astype(jnp.int32),
        "counts": ragged(key_list[3], N_GROUP * N_TILE, N_GROUP * N_TILE * V * 3 // 4, V, 1).astype(jnp.int32),
        "first_weight": noise(key_list[4], (KVOL, C, C), (KVOL * C) ** -0.5, 0.109375),
        "second_weight": noise(key_list[5], (KVOL, C, C), (KVOL * C) ** -0.5, 0.109375),
        "norm_gain": jnp.clip(1.0 + 0.18 * jax.random.normal(key_list[6], (C,), jnp.float32), 0.1, 1.9),
        "cotangent": noise(key_list[7], (N, C), 1.0, 6.0, ((0, 32),)),
    }


def extend(field):
    tiles = field.shape[0]
    chans = field.shape[2]
    before = jnp.concatenate([jnp.zeros((1, F, chans), field.dtype), field[:-1, F:2 * F]], axis=0)
    after = jnp.concatenate([field[1:, :F], jnp.zeros((1, F, chans), field.dtype)], axis=0)
    zero_row = jnp.zeros((tiles, 1, chans), field.dtype)
    return jnp.concatenate([before, field, after, zero_row], axis=1)

def convolve(table, neighbours, weights):
    rows = jnp.take(table, neighbours.T, axis=0)
    gathered = rows.reshape(V, KVOL * C)
    result = jnp.dot(gathered, weights.reshape(KVOL * C, C), preferred_element_type=jnp.float32)
    return (result, gathered)

def convolve_back(gathered, neighbours, weights, grad_out):
    weight_term = lax.dot_general(gathered, grad_out, (((0,), (0,)), ((), ())), preferred_element_type=jnp.float32)
    terms = lax.dot_general(grad_out, weights.reshape(KVOL * C, C), (((1,), (1,)), ((), ())), preferred_element_type=jnp.float32)
    terms = terms.reshape(V * KVOL, C)
    segment_ids = neighbours.T.reshape(-1)
    table_grad = jax.ops.segment_sum(terms, segment_ids, num_segments=V + 2 * F + 1)
    return (weight_term.reshape(KVOL, C, C), table_grad)

def norm_act(first, gain, live):
    centre = lax.optimization_barrier(jnp.mean(first, axis=-1, keepdims=True))
    centred = first - centre
    variance = lax.optimization_barrier(jnp.mean(centred * centred, axis=-1, keepdims=True))
    inv_std = lax.rsqrt(variance + 1e-05)
    unit = centred * inv_std
    normed = unit * gain
    hidden = (jax.nn.gelu(normed) * live).astype(jnp.bfloat16)
    return (hidden, unit, inv_std, normed)

def norm_back(grad_hidden, normed, unit, inv_std, gain, live):
    _, pull = jax.vjp(jax.nn.gelu, normed)
    grad_normed = pull(grad_hidden * live)[0]
    gain_term = lax.optimization_barrier(jnp.sum(grad_normed * unit, axis=0))
    grad_unit = grad_normed * gain
    centred_grad = grad_unit - lax.optimization_barrier(jnp.mean(grad_unit, axis=-1, keepdims=True)) - unit * lax.optimization_barrier(jnp.mean(grad_unit * unit, axis=-1, keepdims=True))
    return ((inv_std * centred_grad).astype(jnp.bfloat16), gain_term)

def fold_tables(table_grad):
    chans = table_grad.shape[2]
    own = table_grad[:, F:F + V]
    from_prev = jnp.concatenate([jnp.zeros((1, F, chans), jnp.float32), table_grad[:-1, V + F:V + 2 * F]], axis=0)
    from_next = jnp.concatenate([table_grad[1:, :F], jnp.zeros((1, F, chans), jnp.float32)], axis=0)
    own = own.at[:, :F].add(from_prev)
    own = own.at[:, F:2 * F].add(from_next)
    return own

def reference(features, kernel_map, send_order, counts, first_weight, second_weight, norm_gain, cotangent):
    tiles = N_GROUP * N_TILE
    per_peer = V // tiles
    feats = features.reshape(tiles, V, C)
    live = (jnp.arange(V, dtype=jnp.int32)[None, :] < counts[:, None]).astype(jnp.float32)[..., None]
    masked = (feats.astype(jnp.float32) * live).astype(jnp.bfloat16)
    table_x = extend(masked)

    def first_layer(inputs):
        table, neighbours, alive = inputs
        first, _ = convolve(table, neighbours, first_weight)
        hidden, _, _, _ = norm_act(first, norm_gain, alive)
        return hidden
    hidden = lax.map(first_layer, (table_x, kernel_map, live))
    table_h = extend(hidden)

    def second_layer(inputs):
        table, neighbours, alive, own = inputs
        second, _ = convolve(table, neighbours, second_weight)
        return ((own.astype(jnp.float32) + second) * alive).astype(jnp.bfloat16)
    block = lax.map(second_layer, (table_h, kernel_map, live, masked))
    ordered = jnp.take_along_axis(block, send_order[:, :, None], axis=1)
    serial_out = ordered.reshape(tiles, tiles, per_peer, C).transpose(1, 0, 2, 3).reshape(tiles * V, C)
    slotted = cotangent.reshape(tiles, tiles, per_peer, C).transpose(1, 0, 2, 3).reshape(tiles, V, C)
    grad_block = jax.vmap(lambda rows, order: jnp.zeros_like(rows).at[order].set(rows))(slotted, send_order)
    grad_live = (grad_block.astype(jnp.float32) * live).astype(jnp.bfloat16)

    def second_back(carry, inputs):
        table, neighbours, grad_out = inputs
        _, gathered = convolve(table, neighbours, second_weight)
        weight_term, table_grad = convolve_back(gathered, neighbours, second_weight, grad_out)
        return (carry + weight_term, table_grad)
    second_grad, table_grad_h = lax.scan(second_back, jnp.zeros((KVOL, C, C), jnp.float32), (table_h, kernel_map, grad_live))
    grad_hidden = fold_tables(table_grad_h)

    def first_back(carry, inputs):
        table, neighbours, alive, grad_h = inputs
        first, gathered = convolve(table, neighbours, first_weight)
        _, unit, inv_std, normed = norm_act(first, norm_gain, alive)
        grad_first, gain_term = norm_back(grad_h, normed, unit, inv_std, norm_gain, alive)
        weight_term, table_grad = convolve_back(gathered, neighbours, first_weight, grad_first)
        return ((carry[0] + weight_term, carry[1] + gain_term), table_grad)
    init = (jnp.zeros((KVOL, C, C), jnp.float32), jnp.zeros((C,), jnp.float32))
    (first_grad, gain_grad), table_grad_x = lax.scan(first_back, init, (table_x, kernel_map, live, grad_hidden))
    grad_x = fold_tables(table_grad_x) + grad_live.astype(jnp.float32)
    grad_features = (grad_x * live).astype(jnp.bfloat16).reshape(tiles * V, C)
    return (serial_out, grad_features, first_grad, second_grad, gain_grad)
```

```python
import jax
import jax.numpy as jnp
from jax import lax
from jax.experimental import pallas as pl
from jax.experimental.pallas import tpu as pltpu
from jax.sharding import PartitionSpec as P

F = 256
B = 256
SHIFT = 8
NT = (((1,), (1,)), ((), ()))
TN = (((0,), (0,)), ((), ()))


def shifted(value, axis, steps):
    count = lax.axis_size(axis)
    initial, last = (max(0, -steps), min(count, count - steps))
    return lax.ppermute(value, axis, [(source, source + steps) for source in range(initial, last)])


def faces_of(field):
    before = shifted(field[F : 2 * F], ("group", "tile"), 1)
    after = shifted(field[:F], ("group", "tile"), -1)
    return before, after


def lane_replicated(row):
    parts = [
        jnp.broadcast_to(row[:, j : j + 128], (128, 128)).T for j in range(0, row.shape[1], 128)
    ]
    return jnp.concatenate(parts, axis=0)


def onehot_rows(index, width):
    lanes = lax.broadcasted_iota(jnp.int32, index.shape, 1)
    parts = [
        jnp.where(index == lanes + j, 1.0, 0.0).astype(jnp.bfloat16) for j in range(0, width, 128)
    ]
    return jnp.concatenate(parts, axis=1)


def onehot_cols(row, height):
    shape = (height, row.shape[1])
    return jnp.where(
        jnp.broadcast_to(row, shape) == lax.broadcasted_iota(jnp.int32, shape, 0), 1.0, 0.0
    ).astype(jnp.bfloat16)


def side_mask(entry, side, slots):
    if side == 0:
        return entry < F
    return (entry >= slots + F) & (entry < slots + 2 * F)


def gather_body(map_ref, field_ref, before_ref, after_ref, weight_ref, *refs, keep):
    if keep:
        rows_ref, out_ref, table_ref = refs
    else:
        out_ref, table_ref = refs
    slots, chans = field_ref.shape
    groups = slots // B
    k = pl.program_id(0)

    @pl.when(k == 0)
    def _():
        out_ref[...] = jnp.zeros_like(out_ref)
        for a in range(groups):
            table_ref[:, a * chans : (a + 1) * chans] = field_ref[a * B : (a + 1) * B, :]

    for block in range(slots // F):
        at = slice(block * F, (block + 1) * F)
        entry = lane_replicated(map_ref[pl.ds(k, 1), at])
        own = entry - F
        low, high = own & (B - 1), own >> SHIFT
        picked = jnp.dot(
            onehot_rows(low, B), table_ref[...], preferred_element_type=jnp.float32
        )
        rows = jnp.where(high == 0, picked[:, :chans], 0.0)
        for a in range(1, groups):
            rows = jnp.where(high == a, picked[:, a * chans : (a + 1) * chans], rows)
        if block < 2:
            face = (before_ref, after_ref)[block][...]
            crossing = jnp.dot(
                onehot_rows(entry & (F - 1), F), face, preferred_element_type=jnp.float32
            )
            rows = jnp.where(side_mask(entry, block, slots), crossing, rows)
        rows = rows.astype(jnp.bfloat16)
        if keep:
            rows_ref[0, at, :] = rows
        out_ref[at, :] += jnp.dot(rows, weight_ref[0], preferred_element_type=jnp.float32)


def resident(shape):
    return pl.BlockSpec(shape, lambda k: (0,) * len(shape))


def per_offset(shape):
    return pl.BlockSpec((1,) + shape, lambda k: (k,) + (0,) * len(shape))


PARAMS = pltpu.CompilerParams(
    dimension_semantics=("arbitrary",), vmem_limit_bytes=56 * 1024 * 1024
)


def gather_convolve(neighbours, field, before, after, weights, keep):
    offsets, slots = neighbours.shape
    chans = field.shape[1]
    out_specs = [resident((slots, chans))]
    out_shape = [jax.ShapeDtypeStruct((slots, chans), jnp.float32)]
    if keep:
        out_specs = [per_offset((slots, chans))] + out_specs
        out_shape = [jax.ShapeDtypeStruct((offsets, slots, chans), jnp.bfloat16)] + out_shape
    return pl.pallas_call(
        lambda *refs: gather_body(*refs, keep=keep),
        grid=(offsets,),
        in_specs=[
            resident((offsets, slots)),
            resident((slots, chans)),
            resident((F, chans)),
            resident((F, chans)),
            per_offset((chans, chans)),
        ],
        out_specs=out_specs,
        out_shape=out_shape,
        scratch_shapes=[pltpu.VMEM((B, slots // B * chans), jnp.bfloat16)],
        compiler_params=PARAMS,
        name="gather_convolve",
    )(neighbours, field, before, after, weights)


def scatter_body(map_ref, grad_ref, weight_ref, *refs, keep):
    if keep:
        sums_ref, out_ref = refs
    else:
        (out_ref,) = refs
    slots, chans = grad_ref.shape
    groups = slots // B
    k = pl.program_id(0)

    @pl.when(k == 0)
    def _():
        out_ref[...] = jnp.zeros_like(out_ref)

    def finish(at, sums):
        sums = sums.astype(jnp.bfloat16)
        if keep:
            sums_ref[0, at, :] = sums
        out_ref[at, :] += lax.dot_general(
            sums, weight_ref[0], NT, preferred_element_type=jnp.float32
        )

    total = None
    for block in range(slots // F):
        at = slice(block * F, (block + 1) * F)
        row = map_ref[pl.ds(k, 1), at]
        entry = lane_replicated(row)
        high = (entry - F) >> SHIFT
        grad = grad_ref[at, :].astype(jnp.float32)
        spread = jnp.concatenate(
            [jnp.where(high == a, grad, 0.0).astype(jnp.bfloat16) for a in range(groups)], axis=1
        )
        term = jnp.dot(
            onehot_cols((row - F) & (B - 1), B), spread, preferred_element_type=jnp.float32
        )
        total = term if total is None else total + term
        if block < 2:
            crossing = jnp.where(side_mask(entry, block, slots), grad, 0.0).astype(jnp.bfloat16)
            start = 0 if block == 0 else slots + F
            finish(
                slice(start, start + F),
                jnp.dot(
                    onehot_cols(row & (F - 1), F), crossing, preferred_element_type=jnp.float32
                ),
            )
    for a in range(groups):
        finish(slice(F + a * B, F + (a + 1) * B), total[:, a * chans : (a + 1) * chans])


def scatter_convolve(neighbours, grad, weights, keep):
    offsets, slots = neighbours.shape
    chans = grad.shape[1]
    rows = slots + 2 * F
    out_specs = [resident((rows, chans))]
    out_shape = [jax.ShapeDtypeStruct((rows, chans), jnp.float32)]
    if keep:
        out_specs = [per_offset((rows, chans))] + out_specs
        out_shape = [jax.ShapeDtypeStruct((offsets, rows, chans), jnp.bfloat16)] + out_shape
    return pl.pallas_call(
        lambda *refs: scatter_body(*refs, keep=keep),
        grid=(offsets,),
        in_specs=[
            resident((offsets, slots)),
            resident((slots, chans)),
            per_offset((chans, chans)),
        ],
        out_specs=out_specs,
        out_shape=out_shape,
        compiler_params=PARAMS,
        name="scatter_convolve",
    )(neighbours, grad, weights)


def weight_body(rows_ref, sums_ref, grad_ref, table_ref, first_ref, second_ref):
    first_ref[0] = lax.dot_general(
        rows_ref[0], grad_ref[...], TN, preferred_element_type=jnp.float32
    )
    second_ref[0] = lax.dot_general(
        table_ref[...], sums_ref[0], TN, preferred_element_type=jnp.float32
    )


def weight_grads(rows, sums, grad, table):
    offsets, slots, chans = rows.shape
    shape = jax.ShapeDtypeStruct((offsets, chans, chans), jnp.float32)
    return pl.pallas_call(
        weight_body,
        grid=(offsets,),
        in_specs=[
            per_offset((slots, chans)),
            per_offset(sums.shape[1:]),
            resident((slots, chans)),
            resident(table.shape),
        ],
        out_specs=[per_offset((chans, chans)), per_offset((chans, chans))],
        out_shape=[shape, shape],
        compiler_params=PARAMS,
        name="weight_grads",
    )(rows, sums, grad, table)


def fold_table(table_grad):
    slots = table_grad.shape[0] - 2 * F
    own = table_grad[F : F + slots]
    from_prev = shifted(
        table_grad[slots + F :].astype(jnp.bfloat16), ("group", "tile"), 1
    ).astype(jnp.float32)
    from_next = shifted(table_grad[:F].astype(jnp.bfloat16), ("group", "tile"), -1).astype(
        jnp.float32
    )
    own = own.at[:F].add(from_prev)
    own = own.at[F : 2 * F].add(from_next)
    return own


def norm_act(first, gain, live):
    centre = jnp.mean(first, axis=-1, keepdims=True)
    centred = first - centre
    variance = jnp.mean(centred * centred, axis=-1, keepdims=True)
    inv_std = lax.rsqrt(variance + 1e-05)
    unit = centred * inv_std
    normed = unit * gain
    hidden = (jax.nn.gelu(normed) * live).astype(jnp.bfloat16)
    return (hidden, unit, inv_std, normed)


def norm_back(grad_hidden, normed, unit, inv_std, gain, live):
    _, pull = jax.vjp(jax.nn.gelu, normed)
    grad_normed = pull(grad_hidden * live)[0]
    gain_term = jnp.sum(grad_normed * unit, axis=0)
    grad_unit = grad_normed * gain
    centred_grad = (
        grad_unit
        - jnp.mean(grad_unit, axis=-1, keepdims=True)
        - unit * jnp.mean(grad_unit * unit, axis=-1, keepdims=True)
    )
    return ((inv_std * centred_grad).astype(jnp.bfloat16), gain_term)


def to_serial(rows):
    return lax.all_to_all(rows, ("group", "tile"), split_axis=0, concat_axis=0, tiled=True)


def to_spatial(rows):
    return lax.all_to_all(rows, ("group", "tile"), split_axis=0, concat_axis=0, tiled=True)


def local(
    features, kernel_map, send_order, counts, first_weight, second_weight, norm_gain, cotangent
):
    slots, chans = features.shape
    neighbours = kernel_map[0]
    order = send_order[0]
    live = (jnp.arange(slots, dtype=jnp.int32) < counts[0]).astype(jnp.float32)[:, None]
    masked = (features.astype(jnp.float32) * live).astype(jnp.bfloat16)
    before_x, after_x = faces_of(masked)
    slotted = to_spatial(cotangent)
    rows_x, first = gather_convolve(neighbours, masked, before_x, after_x, first_weight, True)
    hidden, unit, inv_std, normed = norm_act(first, norm_gain, live)
    before_h, after_h = faces_of(hidden)
    grad_block = jnp.zeros_like(slotted).at[order].set(slotted)
    grad_live = (grad_block.astype(jnp.float32) * live).astype(jnp.bfloat16)
    sums, table_grad_h = scatter_convolve(neighbours, grad_live, second_weight, True)
    grad_hidden = fold_table(table_grad_h)
    grad_first, gain_term = norm_back(grad_hidden, normed, unit, inv_std, norm_gain, live)
    table_h = jnp.concatenate([before_h, hidden, after_h], axis=0)
    first_term, second_term = weight_grads(rows_x, sums, grad_first, table_h)
    first_grad, second_grad, gain_grad = lax.psum(
        (first_term, second_term, gain_term), ("group", "tile")
    )
    (second,) = gather_convolve(neighbours, hidden, before_h, after_h, second_weight, False)
    block = ((masked.astype(jnp.float32) + second) * live).astype(jnp.bfloat16)
    ordered = jnp.take(block, order, axis=0)
    serial_out = to_serial(ordered)
    (table_grad_x,) = scatter_convolve(neighbours, grad_first, first_weight, False)
    grad_x = fold_table(table_grad_x) + grad_live.astype(jnp.float32)
    grad_features = (grad_x * live).astype(jnp.bfloat16)
    return (serial_out, grad_features, first_grad, second_grad, gain_grad)


def solution(mesh):
    placed = (
        P(("group", "tile"), None),
        P(("group", "tile"), None, None),
        P(("group", "tile"), None),
        P(("group", "tile")),
        P(),
        P(),
        P(),
        P(("group", "tile"), None),
    )
    return jax.shard_map(
        local,
        mesh=mesh,
        in_specs=placed,
        out_specs=(P(("group", "tile"), None), P(("group", "tile"), None), P(), P(), P()),
        check_vma=False,
    )
```

```python
import jax
import jax.numpy as jnp
from jax import lax
from jax.experimental import pallas as pl
from jax.experimental.pallas import tpu as pltpu
from jax.sharding import PartitionSpec as P

F = 256
B = 256
SHIFT = 8
WIDE = 1024
EPS = 1e-05
GELU_SCALE = 0.7978845608028654
GELU_CUBIC = 0.044715
AXES = ("group", "tile")
NT = (((1,), (1,)), ((), ()))
PARAMS = pltpu.CompilerParams(
    dimension_semantics=("arbitrary",), vmem_limit_bytes=58 * 1024 * 1024
)


def shifted(value, steps):
    count = lax.axis_size(AXES)
    initial, last = (max(0, -steps), min(count, count - steps))
    return lax.ppermute(value, AXES, [(source, source + steps) for source in range(initial, last)])


def mm(a, b):
    return jnp.dot(a, b, preferred_element_type=jnp.float32)


def lane_replicated(row):
    parts = [
        jnp.broadcast_to(row[:, j : j + 128], (128, 128)).T for j in range(0, row.shape[1], 128)
    ]
    return jnp.concatenate(parts, axis=0)


def onehot_rows(index, width):
    lanes = lax.broadcasted_iota(jnp.int32, index.shape, 1)
    parts = [
        jnp.where(index == lanes + j, 1.0, 0.0).astype(jnp.bfloat16) for j in range(0, width, 128)
    ]
    return jnp.concatenate(parts, axis=1)


def onehot_cols(row, height):
    shape = (height, row.shape[1])
    return jnp.where(
        jnp.broadcast_to(row, shape) == lax.broadcasted_iota(jnp.int32, shape, 0), 1.0, 0.0
    ).astype(jnp.bfloat16)


def side_mask(entry, side, slots):
    if side == 0:
        return entry < F
    return (entry >= slots + F) & (entry < slots + 2 * F)


def alive(start, size, count, chans):
    rows = lax.broadcasted_iota(jnp.int32, (size, chans), 0) + start
    return jnp.where(rows < count, 1.0, 0.0)


def load_table(table_ref, field, start, size, chans):
    for a in range(start // B, (start + size) // B):
        at = a * B - start
        table_ref[:, a * chans : (a + 1) * chans] = field[at : at + B]


def pick(index, table_ref, chans):
    picked = mm(onehot_rows(index & (B - 1), B), table_ref[...])
    high = index >> SHIFT
    rows = jnp.where(high == 0, picked[:, :chans], 0.0)
    for a in range(1, table_ref.shape[1] // chans):
        rows = jnp.where(high == a, picked[:, a * chans : (a + 1) * chans], rows)
    return rows


def drop(row, index, value, groups):
    high = index >> SHIFT
    spread = jnp.concatenate(
        [jnp.where(high == a, value, 0.0).astype(jnp.bfloat16) for a in range(groups)], axis=1
    )
    return mm(onehot_cols(row & (B - 1), B), spread)


def normalise(first, gain):
    centred = first - jnp.mean(first, axis=-1, keepdims=True)
    inv_std = lax.rsqrt(jnp.mean(centred * centred, axis=-1, keepdims=True) + EPS)
    unit = centred * inv_std
    normed = unit * gain
    bent = jnp.tanh(GELU_SCALE * (normed + GELU_CUBIC * (normed * normed * normed)))
    return unit, inv_std, normed, bent


def gather_step(map_ref, before_ref, after_ref, weight_ref, out_ref, table_ref, slots, chans):
    step = pl.program_id(0)
    unroll = weight_ref.shape[0]
    weight = weight_ref[...].reshape(unroll * chans, chans)
    for start in range(0, slots, WIDE):
        size = min(WIDE, slots - start)
        found = []
        for u in range(unroll):
            entry = lane_replicated(map_ref[pl.ds(step * unroll + u, 1), start : start + size])
            rows = pick(entry - F, table_ref, chans)
            parts = []
            for side, face_ref in enumerate((before_ref, after_ref)):
                at = side * F - start
                if 0 <= at < size:
                    near = entry[at : at + F]
                    crossing = mm(onehot_rows(near & (F - 1), F), face_ref[...])
                    parts.append(
                        jnp.where(side_mask(near, side, slots), crossing, rows[at : at + F])
                    )
            if parts:
                parts.append(rows[len(parts) * F :])
                rows = jnp.concatenate(parts, axis=0)
            found.append(rows.astype(jnp.bfloat16))
        out_ref[start : start + size, :] += mm(jnp.concatenate(found, axis=1), weight)


def first_layer_body(
    count_ref, map_ref, field_ref, before_ref, after_ref, weight_ref, gain_ref,
    first_ref, hidden_ref, table_ref,
):
    slots, chans = field_ref.shape
    step = pl.program_id(0)

    @pl.when(step == 0)
    def _():
        first_ref[...] = jnp.zeros_like(first_ref)
        for start in range(0, slots, B):
            field = field_ref[start : start + B, :].astype(jnp.float32)
            field = (field * alive(start, B, count_ref[0], chans)).astype(jnp.bfloat16)
            load_table(table_ref, field, start, B, chans)

    gather_step(map_ref, before_ref, after_ref, weight_ref, first_ref, table_ref, slots, chans)

    @pl.when(step == pl.num_programs(0) - 1)
    def _():
        for start in range(0, slots, B):
            at = slice(start, start + B)
            _, _, normed, bent = normalise(first_ref[at, :], gain_ref[...])
            act = 0.5 * normed * (1.0 + bent)
            hidden_ref[at, :] = (act * alive(start, B, count_ref[0], chans)).astype(jnp.bfloat16)


def second_layer_body(
    count_ref, map_ref, order_ref, skip_ref, field_ref, before_ref, after_ref, weight_ref,
    serial_ref, second_ref, table_ref,
):
    slots, chans = field_ref.shape
    step = pl.program_id(0)

    @pl.when(step == 0)
    def _():
        second_ref[...] = jnp.zeros_like(second_ref)
        load_table(table_ref, field_ref, 0, slots, chans)

    gather_step(map_ref, before_ref, after_ref, weight_ref, second_ref, table_ref, slots, chans)

    @pl.when(step == pl.num_programs(0) - 1)
    def _():
        for start in range(0, slots, B):
            at = slice(start, start + B)
            live = alive(start, B, count_ref[0], chans)
            masked = skip_ref[at, :].astype(jnp.float32) * live
            block = ((masked + second_ref[at, :]) * live).astype(jnp.bfloat16)
            load_table(table_ref, block, start, B, chans)
        for start in range(0, slots, WIDE):
            size = min(WIDE, slots - start)
            index = lane_replicated(order_ref[:, start : start + size])
            serial_ref[start : start + size, :] = pick(index, table_ref, chans).astype(
                jnp.bfloat16
            )


def scatter_step(map_ref, weight_ref, grad_ref, turned_ref, total_ref, wgrad_ref):
    slots, chans = grad_ref.shape
    groups = slots // B
    step = pl.program_id(0)
    unroll = weight_ref.shape[0]
    near, own = [], []
    for u in range(unroll):
        row = map_ref[pl.ds(step * unroll + u, 1), :]
        entry = lane_replicated(row)
        grad = grad_ref[...].astype(jnp.float32)
        own.append(drop(row - F, entry - F, grad, groups).astype(jnp.bfloat16))
        faces = []
        for side in range(2):
            at = slice(side * F, (side + 1) * F)
            crossing = jnp.where(side_mask(entry[at], side, slots), grad[at], 0.0)
            faces.append(
                mm(onehot_cols(row[:, at] & (F - 1), F), crossing.astype(jnp.bfloat16)).astype(
                    jnp.bfloat16
                )
            )
        near.append(faces)
    back = jnp.concatenate([weight_ref[u] for u in range(unroll)], axis=1)
    wide = None
    starts = [0] + [F + a * B for a in range(groups)] + [F + slots]
    for n, start in enumerate(starts):
        if 0 < n <= groups:
            a = n - 1
            piece = [own[u][:, a * chans : (a + 1) * chans] for u in range(unroll)]
        else:
            piece = [near[u][0 if n == 0 else 1] for u in range(unroll)]
        piece = jnp.concatenate(piece, axis=1)
        at = slice(start, start + piece.shape[0])
        total_ref[at, :] += lax.dot_general(piece, back, NT, preferred_element_type=jnp.float32)
        term = mm(turned_ref[:, at], piece)
        wide = term if wide is None else wide + term
    for u in range(unroll):
        wgrad_ref[step * unroll + u] = wide[:, u * chans : (u + 1) * chans]


def turn_table(turned_ref, before, own, after):
    slots = own.shape[0]
    turned_ref[:, :F] = before.T
    turned_ref[:, F : F + slots] = own.T
    turned_ref[:, F + slots :] = after.T


def give_back(total_ref, own_ref, prev_ref, next_ref):
    slots = own_ref.shape[0]
    own_ref[...] = total_ref[F : F + slots, :]
    prev_ref[...] = total_ref[:F, :].astype(jnp.bfloat16)
    next_ref[...] = total_ref[F + slots :, :].astype(jnp.bfloat16)


def second_back_body(
    count_ref, map_ref, order_ref, slotted_ref, field_ref, before_ref, after_ref, weight_ref,
    own_ref, prev_ref, next_ref, wgrad_ref, grad_ref, turned_ref, total_ref,
):
    slots, chans = field_ref.shape
    step = pl.program_id(0)

    @pl.when(step == 0)
    def _():
        total_ref[...] = jnp.zeros_like(total_ref)
        turn_table(turned_ref, before_ref[...], field_ref[...], after_ref[...])
        order = order_ref[...]
        placed = drop(
            order, lane_replicated(order), slotted_ref[...].astype(jnp.float32), slots // B
        )
        for a in range(slots // B):
            live = alive(a * B, B, count_ref[0], chans)
            grad_ref[a * B : (a + 1) * B, :] = (
                placed[:, a * chans : (a + 1) * chans] * live
            ).astype(jnp.bfloat16)

    scatter_step(map_ref, weight_ref, grad_ref, turned_ref, total_ref, wgrad_ref)

    @pl.when(step == pl.num_programs(0) - 1)
    def _():
        give_back(total_ref, own_ref, prev_ref, next_ref)


def first_back_body(
    count_ref, map_ref, first_ref, upper_ref, from_prev_ref, from_next_ref, gain_ref,
    field_ref, before_ref, after_ref, weight_ref,
    own_ref, prev_ref, next_ref, wgrad_ref, grad_ref, turned_ref, total_ref,
):
    slots, chans = field_ref.shape
    step = pl.program_id(0)

    @pl.when(step == 0)
    def _():
        total_ref[...] = jnp.zeros_like(total_ref)
        gain_term = jnp.zeros((1, chans), jnp.float32)
        turned_ref[:, :F] = before_ref[...].T
        turned_ref[:, F + slots :] = after_ref[...].T
        for start in range(0, slots, B):
            at = slice(start, start + B)
            live = alive(start, B, count_ref[0], chans)
            masked = (field_ref[at, :].astype(jnp.float32) * live).astype(jnp.bfloat16)
            turned_ref[:, F + start : F + start + B] = masked.T
            upper = upper_ref[at, :]
            if start == 0:
                upper = upper + from_prev_ref[...].astype(jnp.float32)
            if start == F:
                upper = upper + from_next_ref[...].astype(jnp.float32)
            unit, inv_std, normed, bent = normalise(first_ref[at, :], gain_ref[...])
            inner = GELU_SCALE * (1.0 + 3.0 * GELU_CUBIC * (normed * normed))
            slope = 0.5 * (1.0 + bent) + 0.5 * normed * (1.0 - bent * bent) * inner
            grad_normed = slope * (upper * live)
            gain_term = gain_term + jnp.sum(grad_normed * unit, axis=0, keepdims=True)
            grad_unit = grad_normed * gain_ref[...]
            centred = (
                grad_unit
                - jnp.mean(grad_unit, axis=-1, keepdims=True)
                - unit * jnp.mean(grad_unit * unit, axis=-1, keepdims=True)
            )
            grad_ref[at, :] = (inv_std * centred).astype(jnp.bfloat16)
        lanes = lax.broadcasted_iota(jnp.int32, (chans, chans), 0)
        wgrad_ref[wgrad_ref.shape[0] - 1] = jnp.where(
            lanes == 0, jnp.broadcast_to(gain_term, (chans, chans)), 0.0
        )

    scatter_step(map_ref, weight_ref, grad_ref, turned_ref, total_ref, wgrad_ref)

    @pl.when(step == pl.num_programs(0) - 1)
    def _():
        give_back(total_ref, own_ref, prev_ref, next_ref)


def call(body, name, operands, stepped, outputs, scratch):
    offsets = operands[stepped].shape[0]
    unroll = 3 if offsets % 3 == 0 else 1

    def whole(shape):
        return pl.BlockSpec(shape, lambda k: (0,) * len(shape))

    specs = []
    for n, operand in enumerate(operands):
        if n == 0:
            specs.append(pl.BlockSpec(memory_space=pltpu.SMEM))
        elif n == stepped:
            specs.append(pl.BlockSpec((unroll,) + operand.shape[1:], lambda k: (k, 0, 0)))
        else:
            specs.append(whole(operand.shape))
    return pl.pallas_call(
        body,
        grid=(offsets // unroll,),
        in_specs=specs,
        out_specs=[whole(shape) for shape, _ in outputs],
        out_shape=[jax.ShapeDtypeStruct(shape, dtype) for shape, dtype in outputs],
        scratch_shapes=[pltpu.VMEM(shape, dtype) for shape, dtype in scratch],
        compiler_params=PARAMS,
        name=name,
    )(*operands)


def swap_rows(rows):
    return lax.all_to_all(rows, AXES, split_axis=0, concat_axis=0, tiled=True)


def local(
    features, kernel_map, send_order, counts, first_weight, second_weight, norm_gain, cotangent
):
    slots, chans = features.shape
    neighbours = kernel_map[0]
    offsets = neighbours.shape[0]
    gain = norm_gain[None, :]
    bf16, f32 = jnp.bfloat16, jnp.float32
    rows16, rows32 = ((slots, chans), bf16), ((slots, chans), f32)
    face16 = ((F, chans), bf16)
    table16 = ((B, slots // B * chans), bf16)
    turned16 = ((chans, slots + 2 * F), bf16)
    total32 = ((slots + 2 * F, chans), f32)

    ends = jnp.arange(2 * F, dtype=jnp.int32)[:, None] < counts[0]
    ends_x = (features[: 2 * F].astype(f32) * ends.astype(f32)).astype(bf16)
    before_x, after_x = shifted(ends_x[F:], 1), shifted(ends_x[:F], -1)
    slotted = swap_rows(cotangent)
    first, hidden = call(
        first_layer_body, "first_layer",
        (counts, neighbours, features, before_x, after_x, first_weight, gain), 5,
        (rows32, rows16), (table16,),
    )
    before_h, after_h = shifted(hidden[F : 2 * F], 1), shifted(hidden[:F], -1)
    upper, upper_prev, upper_next, second_term, grad_live = call(
        second_back_body, "second_back",
        (counts, neighbours, send_order, slotted, hidden, before_h, after_h, second_weight), 7,
        (rows32, face16, face16, ((offsets, chans, chans), f32), rows16), (turned16, total32),
    )
    second_grad = lax.psum(second_term, AXES)
    from_prev, from_next = shifted(upper_next, 1), shifted(upper_prev, -1)
    lower, lower_prev, lower_next, first_term = call(
        first_back_body, "first_back",
        (counts, neighbours, first, upper, from_prev, from_next, gain, features, before_x,
         after_x, first_weight), 10,
        (rows32, face16, face16, ((offsets + 1, chans, chans), f32)),
        (rows16, turned16, total32),
    )
    reduced = lax.psum(first_term, ("tile", "group"))
    down_prev, down_next = shifted(lower_next, 1), shifted(lower_prev, -1)
    (ordered,) = call(
        second_layer_body, "second_layer",
        (counts, neighbours, send_order, features, hidden, before_h, after_h, second_weight), 7,
        (rows16,), (rows32, table16),
    )
    serial_out = swap_rows(ordered)
    live = (jnp.arange(slots, dtype=jnp.int32) < counts[0]).astype(f32)[:, None]
    grad_x = lower + grad_live.astype(f32)
    grad_x = grad_x.at[:F].add(down_prev.astype(f32))
    grad_x = grad_x.at[F : 2 * F].add(down_next.astype(f32))
    grad_features = (grad_x * live).astype(bf16)
    return (serial_out, grad_features, reduced[:offsets], second_grad, reduced[offsets, 0])


def solution(mesh):
    placed = (
        P(AXES, None),
        P(AXES, None, None),
        P(AXES, None),
        P(AXES),
        P(),
        P(),
        P(),
        P(AXES, None),
    )
    return jax.shard_map(
        local,
        mesh=mesh,
        in_specs=placed,
        out_specs=(P(AXES, None), P(AXES, None), P(), P(), P()),
        check_vma=False,
    )
```

```python
import jax
import jax.numpy as jnp
from jax import lax
from jax.experimental import pallas as pl
from jax.experimental.pallas import tpu as pltpu
from jax.sharding import PartitionSpec as P

F = 256
B = 256
SHIFT = 8
WIDE = 1024
EPS = 1e-05
GELU_SCALE = 0.7978845608028654
GELU_CUBIC = 0.044715
AXES = ("group", "tile")
NT = (((1,), (1,)), ((), ()))
PARAMS = pltpu.CompilerParams(
    dimension_semantics=("arbitrary",), vmem_limit_bytes=58 * 1024 * 1024
)


def shifted(value, steps):
    count = lax.axis_size(AXES)
    initial, last = (max(0, -steps), min(count, count - steps))
    return lax.ppermute(value, AXES, [(source, source + steps) for source in range(initial, last)])


def mm(a, b):
    return jnp.dot(a, b, preferred_element_type=jnp.float32)


def lane_replicated(row):
    parts = [
        jnp.broadcast_to(row[:, j : j + 128], (128, 128)).T for j in range(0, row.shape[1], 128)
    ]
    return jnp.concatenate(parts, axis=0)


def onehot_rows(index, width):
    lanes = lax.broadcasted_iota(jnp.int32, index.shape, 1)
    parts = [
        jnp.where(index == lanes + j, 1.0, 0.0).astype(jnp.bfloat16) for j in range(0, width, 128)
    ]
    return jnp.concatenate(parts, axis=1)


def onehot_cols(row, height):
    shape = (height, row.shape[1])
    return jnp.where(
        jnp.broadcast_to(row, shape) == lax.broadcasted_iota(jnp.int32, shape, 0), 1.0, 0.0
    ).astype(jnp.bfloat16)


def side_mask(entry, side, slots):
    if side == 0:
        return entry < F
    return (entry >= slots + F) & (entry < slots + 2 * F)


def alive(start, size, count, chans):
    rows = lax.broadcasted_iota(jnp.int32, (size, chans), 0) + start
    return jnp.where(rows < count, 1.0, 0.0)


def load_table(table_ref, field, start, size, chans):
    for a in range(start // B, (start + size) // B):
        at = a * B - start
        table_ref[:, a * chans : (a + 1) * chans] = field[at : at + B]


def pick(index, table_ref, chans):
    picked = mm(onehot_rows(index & (B - 1), B), table_ref[...])
    high = index >> SHIFT
    rows = jnp.where(high == 0, picked[:, :chans], 0.0)
    for a in range(1, table_ref.shape[1] // chans):
        rows = jnp.where(high == a, picked[:, a * chans : (a + 1) * chans], rows)
    return rows


def drop(row, index, value, groups):
    high = index >> SHIFT
    spread = jnp.concatenate(
        [jnp.where(high == a, value, 0.0).astype(jnp.bfloat16) for a in range(groups)], axis=1
    )
    return mm(onehot_cols(row & (B - 1), B), spread)


def normalise(first, gain):
    centred = first - jnp.mean(first, axis=-1, keepdims=True)
    inv_std = lax.rsqrt(jnp.mean(centred * centred, axis=-1, keepdims=True) + EPS)
    unit = centred * inv_std
    normed = unit * gain
    bent = jnp.tanh(GELU_SCALE * (normed + GELU_CUBIC * (normed * normed * normed)))
    return unit, inv_std, normed, bent


def gather_step(
    map_ref, before_ref, after_ref, weight_ref, out_ref, table_ref, slots, chans, keep_ref=None
):
    step = pl.program_id(0)
    unroll = weight_ref.shape[0]
    weight = weight_ref[...].reshape(unroll * chans, chans)
    for start in range(0, slots, WIDE):
        size = min(WIDE, slots - start)
        found = []
        for u in range(unroll):
            entry = lane_replicated(map_ref[pl.ds(step * unroll + u, 1), start : start + size])
            rows = pick(entry - F, table_ref, chans)
            parts = []
            for side, face_ref in enumerate((before_ref, after_ref)):
                at = side * F - start
                if 0 <= at < size:
                    near = entry[at : at + F]
                    crossing = mm(onehot_rows(near & (F - 1), F), face_ref[...])
                    parts.append(
                        jnp.where(side_mask(near, side, slots), crossing, rows[at : at + F])
                    )
            if parts:
                parts.append(rows[len(parts) * F :])
                rows = jnp.concatenate(parts, axis=0)
            found.append(rows.astype(jnp.bfloat16))
            if keep_ref is not None:
                keep_ref[u, start : start + size, :] = found[-1]
        out_ref[start : start + size, :] += mm(jnp.concatenate(found, axis=1), weight)


def first_layer_body(
    count_ref, map_ref, field_ref, before_ref, after_ref, weight_ref, gain_ref,
    first_ref, hidden_ref, rows_ref, table_ref,
):
    slots, chans = field_ref.shape
    step = pl.program_id(0)

    @pl.when(step == 0)
    def _():
        first_ref[...] = jnp.zeros_like(first_ref)
        for start in range(0, slots, B):
            field = field_ref[start : start + B, :].astype(jnp.float32)
            field = (field * alive(start, B, count_ref[0], chans)).astype(jnp.bfloat16)
            load_table(table_ref, field, start, B, chans)

    gather_step(
        map_ref, before_ref, after_ref, weight_ref, first_ref, table_ref, slots, chans, rows_ref
    )

    @pl.when(step == pl.num_programs(0) - 1)
    def _():
        for start in range(0, slots, B):
            at = slice(start, start + B)
            _, _, normed, bent = normalise(first_ref[at, :], gain_ref[...])
            act = 0.5 * normed * (1.0 + bent)
            hidden_ref[at, :] = (act * alive(start, B, count_ref[0], chans)).astype(jnp.bfloat16)


def second_layer_body(
    count_ref, map_ref, order_ref, skip_ref, field_ref, before_ref, after_ref, weight_ref,
    serial_ref, second_ref, table_ref,
):
    slots, chans = field_ref.shape
    step = pl.program_id(0)

    @pl.when(step == 0)
    def _():
        second_ref[...] = jnp.zeros_like(second_ref)
        load_table(table_ref, field_ref, 0, slots, chans)

    gather_step(map_ref, before_ref, after_ref, weight_ref, second_ref, table_ref, slots, chans)

    @pl.when(step == pl.num_programs(0) - 1)
    def _():
        for start in range(0, slots, B):
            at = slice(start, start + B)
            live = alive(start, B, count_ref[0], chans)
            masked = skip_ref[at, :].astype(jnp.float32) * live
            block = ((masked + second_ref[at, :]) * live).astype(jnp.bfloat16)
            load_table(table_ref, block, start, B, chans)
        for start in range(0, slots, WIDE):
            size = min(WIDE, slots - start)
            index = lane_replicated(order_ref[:, start : start + size])
            serial_ref[start : start + size, :] = pick(index, table_ref, chans).astype(
                jnp.bfloat16
            )


def scatter_step(map_ref, weight_ref, grad_ref, total_ref, near_ref=None, turned_ref=None, wgrad_ref=None):
    slots, chans = grad_ref.shape
    groups = slots // B
    step = pl.program_id(0)
    unroll = weight_ref.shape[0]
    near, own = [], []
    for u in range(unroll):
        row = map_ref[pl.ds(step * unroll + u, 1), :]
        entry = lane_replicated(row)
        grad = grad_ref[...].astype(jnp.float32)
        own.append(drop(row - F, entry - F, grad, groups).astype(jnp.bfloat16))
        faces = []
        for side in range(2):
            at = slice(side * F, (side + 1) * F)
            crossing = jnp.where(side_mask(entry[at], side, slots), grad[at], 0.0)
            faces.append(
                mm(onehot_cols(row[:, at] & (F - 1), F), crossing.astype(jnp.bfloat16)).astype(
                    jnp.bfloat16
                )
            )
            if near_ref is not None:
                near_ref[u, at, :] = faces[-1]
        near.append(faces)
    back = jnp.concatenate([weight_ref[u] for u in range(unroll)], axis=1)
    wide = None
    starts = [0] + [F + a * B for a in range(groups)] + [F + slots]
    for n, start in enumerate(starts):
        inside = 0 < n <= groups
        if inside:
            a = n - 1
            piece = [own[u][:, a * chans : (a + 1) * chans] for u in range(unroll)]
        else:
            piece = [near[u][0 if n == 0 else 1] for u in range(unroll)]
        piece = jnp.concatenate(piece, axis=1)
        at = slice(start, start + piece.shape[0])
        total_ref[at, :] += lax.dot_general(piece, back, NT, preferred_element_type=jnp.float32)
        if inside and wgrad_ref is not None:
            term = mm(turned_ref[:, a * B : (a + 1) * B], piece)
            wide = term if wide is None else wide + term
    if wgrad_ref is not None:
        for u in range(unroll):
            wgrad_ref[u] = wide[:, u * chans : (u + 1) * chans]


def give_back(total_ref, own_ref, prev_ref, next_ref):
    slots = own_ref.shape[0]
    own_ref[...] = total_ref[F : F + slots, :]
    prev_ref[...] = total_ref[:F, :].astype(jnp.bfloat16)
    next_ref[...] = total_ref[F + slots :, :].astype(jnp.bfloat16)


def second_back_body(
    count_ref, map_ref, order_ref, slotted_ref, field_ref, weight_ref,
    own_ref, prev_ref, next_ref, wgrad_ref, near_ref, grad_ref, turned_ref, total_ref,
):
    slots, chans = field_ref.shape
    step = pl.program_id(0)

    @pl.when(step == 0)
    def _():
        total_ref[...] = jnp.zeros_like(total_ref)
        turned_ref[...] = field_ref[...].T
        order = order_ref[...]
        placed = drop(
            order, lane_replicated(order), slotted_ref[...].astype(jnp.float32), slots // B
        )
        for a in range(slots // B):
            live = alive(a * B, B, count_ref[0], chans)
            grad_ref[a * B : (a + 1) * B, :] = (
                placed[:, a * chans : (a + 1) * chans] * live
            ).astype(jnp.bfloat16)

    scatter_step(map_ref, weight_ref, grad_ref, total_ref, near_ref, turned_ref, wgrad_ref)

    @pl.when(step == pl.num_programs(0) - 1)
    def _():
        give_back(total_ref, own_ref, prev_ref, next_ref)


def weights_body(
    count_ref, first_ref, upper_ref, from_prev_ref, from_next_ref, gain_ref,
    before_ref, after_ref, rows_ref, near_ref, partial_ref,
    grad_ref, wgrad_ref, turned_ref, faces_ref,
):
    slots, chans = first_ref.shape
    step = pl.program_id(0)
    unroll = rows_ref.shape[0]
    half = wgrad_ref.shape[0] // 2

    @pl.when(step == 0)
    def _():
        gain_term = jnp.zeros((1, chans), jnp.float32)
        faces_ref[:, :F] = before_ref[...].T
        faces_ref[:, F:] = after_ref[...].T
        for start in range(0, slots, B):
            at = slice(start, start + B)
            live = alive(start, B, count_ref[0], chans)
            upper = upper_ref[at, :]
            if start == 0:
                upper = upper + from_prev_ref[...].astype(jnp.float32)
            if start == F:
                upper = upper + from_next_ref[...].astype(jnp.float32)
            unit, inv_std, normed, bent = normalise(first_ref[at, :], gain_ref[...])
            inner = GELU_SCALE * (1.0 + 3.0 * GELU_CUBIC * (normed * normed))
            slope = 0.5 * (1.0 + bent) + 0.5 * normed * (1.0 - bent * bent) * inner
            grad_normed = slope * (upper * live)
            gain_term = gain_term + jnp.sum(grad_normed * unit, axis=0, keepdims=True)
            grad_unit = grad_normed * gain_ref[...]
            centred = (
                grad_unit
                - jnp.mean(grad_unit, axis=-1, keepdims=True)
                - unit * jnp.mean(grad_unit * unit, axis=-1, keepdims=True)
            )
            grad = (inv_std * centred).astype(jnp.bfloat16)
            grad_ref[at, :] = grad
            turned_ref[:, at] = grad.T
        row = lax.broadcasted_iota(jnp.int32, (chans, chans), 0)
        high = gain_term.astype(jnp.bfloat16).astype(jnp.float32)
        wgrad_ref[half - 1] = jnp.where(
            row == 0, high, jnp.where(row == 1, gain_term - high, 0.0)
        ).astype(jnp.bfloat16)
        wgrad_ref[2 * half - 1] = jnp.zeros((chans, chans), jnp.bfloat16)

    wide = mm(turned_ref[...], jnp.concatenate([rows_ref[u] for u in range(unroll)], axis=1))
    edge = mm(faces_ref[...], jnp.concatenate([near_ref[u] for u in range(unroll)], axis=1))
    for u in range(unroll):
        at = slice(u * chans, (u + 1) * chans)
        wgrad_ref[step * unroll + u] = wide[:, at].T.astype(jnp.bfloat16)
        wgrad_ref[half + step * unroll + u] = (partial_ref[u] + edge[:, at]).astype(jnp.bfloat16)


def first_back_body(
    count_ref, map_ref, grad_ref, weight_ref, own_ref, prev_ref, next_ref, total_ref
):
    step = pl.program_id(0)

    @pl.when(step == 0)
    def _():
        total_ref[...] = jnp.zeros_like(total_ref)

    scatter_step(map_ref, weight_ref, grad_ref, total_ref)

    @pl.when(step == pl.num_programs(0) - 1)
    def _():
        give_back(total_ref, own_ref, prev_ref, next_ref)


def call(body, name, operands, stepped, outputs, scratch):
    offsets = operands[stepped[0]].shape[0]
    unroll = 3 if offsets % 3 == 0 else 1

    def spec(shape, cut):
        if cut:
            return pl.BlockSpec((unroll,) + shape[1:], lambda k: (k,) + (0,) * (len(shape) - 1))
        return pl.BlockSpec(shape, lambda k: (0,) * len(shape))

    specs = [pl.BlockSpec(memory_space=pltpu.SMEM)]
    specs += [spec(o.shape, n in stepped) for n, o in enumerate(operands) if n > 0]
    return pl.pallas_call(
        body,
        grid=(offsets // unroll,),
        in_specs=specs,
        out_specs=[spec(out[0], len(out) > 2) for out in outputs],
        out_shape=[jax.ShapeDtypeStruct(out[0], out[1]) for out in outputs],
        scratch_shapes=[pltpu.VMEM(shape, dtype) for shape, dtype in scratch],
        compiler_params=PARAMS,
        name=name,
    )(*operands)


def swap_rows(rows):
    return lax.all_to_all(rows, AXES, split_axis=0, concat_axis=0, tiled=True)


def local(
    features, kernel_map, send_order, counts, first_weight, second_weight, norm_gain, cotangent
):
    slots, chans = features.shape
    neighbours = kernel_map[0]
    offsets = neighbours.shape[0]
    devices = lax.axis_size(AXES)
    gain = norm_gain[None, :]
    bf16, f32 = jnp.bfloat16, jnp.float32
    rows16, rows32 = ((slots, chans), bf16), ((slots, chans), f32)
    face16 = ((F, chans), bf16)
    table16 = ((B, slots // B * chans), bf16)
    turned16 = ((chans, slots), bf16)
    total32 = ((slots + 2 * F, chans), f32)

    ends = jnp.arange(2 * F, dtype=jnp.int32)[:, None] < counts[0]
    ends_x = (features[: 2 * F].astype(f32) * ends.astype(f32)).astype(bf16)
    before_x, after_x = shifted(ends_x[F:], 1), shifted(ends_x[:F], -1)
    slotted = swap_rows(cotangent)
    first, hidden, rows_x = call(
        first_layer_body, "first_layer",
        (counts, neighbours, features, before_x, after_x, first_weight, gain), (5,),
        (rows32, rows16, ((offsets, slots, chans), bf16, True)), (table16,),
    )
    before_h, after_h = shifted(hidden[F : 2 * F], 1), shifted(hidden[:F], -1)
    upper, upper_prev, upper_next, partial, near, grad_live = call(
        second_back_body, "second_back",
        (counts, neighbours, send_order, slotted, hidden, second_weight), (5,),
        (rows32, face16, face16, ((offsets, chans, chans), f32, True),
         ((offsets, 2 * F, chans), bf16, True), rows16),
        (turned16, total32),
    )
    from_prev, from_next = shifted(upper_next, 1), shifted(upper_prev, -1)
    grad_first, wgrads = call(
        weights_body, "weights",
        (counts, first, upper, from_prev, from_next, gain, before_h, after_h, rows_x, near,
         partial), (8, 9, 10),
        (rows16, ((2 * (offsets + 1), chans, chans), bf16)), (turned16, ((chans, 2 * F), bf16)),
    )
    parts = swap_rows(wgrads.reshape(devices, -1, chans))
    hidden, grad_first = lax.optimization_barrier((hidden, grad_first))
    (ordered,) = call(
        second_layer_body, "second_layer",
        (counts, neighbours, send_order, features, hidden, before_h, after_h, second_weight),
        (7,), (rows16,), (rows32, table16),
    )
    part = jnp.sum(parts.astype(f32), axis=0).astype(bf16)
    ordered, part, grad_first = lax.optimization_barrier((ordered, part, grad_first))
    per_peer = slots // devices
    both = swap_rows(
        jnp.concatenate(
            [
                ordered.reshape(devices, per_peer, chans),
                jnp.broadcast_to(part[None], (devices,) + part.shape),
            ],
            axis=1,
        )
    )
    serial_out = both[:, :per_peer].reshape(slots, chans)
    shared = both[:, per_peer:]
    lower, lower_prev, lower_next = call(
        first_back_body, "first_back",
        (counts, neighbours, grad_first, first_weight), (3,),
        (rows32, face16, face16), (total32,),
    )
    down_prev, down_next = shifted(lower_next, 1), shifted(lower_prev, -1)
    live = (jnp.arange(slots, dtype=jnp.int32) < counts[0]).astype(f32)[:, None]
    grad_x = lower + grad_live.astype(f32)
    grad_x = grad_x.at[:F].add(down_prev.astype(f32))
    grad_x = grad_x.at[F : 2 * F].add(down_next.astype(f32))
    grad_features = (grad_x * live).astype(bf16)
    shared = shared.reshape(2, offsets + 1, chans, chans)
    first_grad, second_grad = shared[0, :offsets].astype(f32), shared[1, :offsets].astype(f32)
    gain_grad = shared[0, offsets, 0].astype(f32) + shared[0, offsets, 1].astype(f32)
    return (serial_out, grad_features, first_grad, second_grad, gain_grad)


def solution(mesh):
    placed = (
        P(AXES, None),
        P(AXES, None, None),
        P(AXES, None),
        P(AXES),
        P(),
        P(),
        P(),
        P(AXES, None),
    )
    return jax.shard_map(
        local,
        mesh=mesh,
        in_specs=placed,
        out_specs=(P(AXES, None), P(AXES, None), P(), P(), P()),
        check_vma=False,
    )
```

```python
import jax
import jax.numpy as jnp
from jax import lax
from jax.experimental import pallas as pl
from jax.experimental.pallas import tpu as pltpu
from jax.sharding import PartitionSpec as P

F = 256
B = 256
SHIFT = 8
WIDE = 1024
EPS = 1e-05
GELU_SCALE = 0.7978845608028654
GELU_CUBIC = 0.044715
AXES = ("group", "tile")
NT = (((1,), (1,)), ((), ()))
PARAMS = pltpu.CompilerParams(
    dimension_semantics=("arbitrary",), vmem_limit_bytes=58 * 1024 * 1024
)


def shifted(value, steps):
    count = lax.axis_size(AXES)
    initial, last = (max(0, -steps), min(count, count - steps))
    return lax.ppermute(value, AXES, [(source, source + steps) for source in range(initial, last)])


def mm(a, b):
    return jnp.dot(a, b, preferred_element_type=jnp.float32)


def lane_replicated(row):
    parts = [
        jnp.broadcast_to(row[:, j : j + 128], (128, 128)).T for j in range(0, row.shape[1], 128)
    ]
    return jnp.concatenate(parts, axis=0)


def onehot_rows(index, width):
    lanes = lax.broadcasted_iota(jnp.int32, index.shape, 1)
    parts = [
        jnp.where(index == lanes + j, 1.0, 0.0).astype(jnp.bfloat16) for j in range(0, width, 128)
    ]
    return jnp.concatenate(parts, axis=1)


def onehot_cols(row, height):
    shape = (height, row.shape[1])
    return jnp.where(
        jnp.broadcast_to(row, shape) == lax.broadcasted_iota(jnp.int32, shape, 0), 1.0, 0.0
    ).astype(jnp.bfloat16)


def side_mask(entry, side, slots):
    if side == 0:
        return entry < F
    return (entry >= slots + F) & (entry < slots + 2 * F)


def alive(start, size, count, chans):
    rows = lax.broadcasted_iota(jnp.int32, (size, chans), 0) + start
    return jnp.where(rows < count, 1.0, 0.0)


def load_table(table_ref, field, start, size, chans):
    for a in range(start // B, (start + size) // B):
        at = a * B - start
        table_ref[:, a * chans : (a + 1) * chans] = field[at : at + B]


def pick(index, table_ref, chans):
    picked = mm(onehot_rows(index & (B - 1), B), table_ref[...])
    high = index >> SHIFT
    rows = jnp.where(high == 0, picked[:, :chans], 0.0)
    for a in range(1, table_ref.shape[1] // chans):
        rows = jnp.where(high == a, picked[:, a * chans : (a + 1) * chans], rows)
    return rows


def drop(row, index, value, groups):
    high = index >> SHIFT
    spread = jnp.concatenate(
        [jnp.where(high == a, value, 0.0).astype(jnp.bfloat16) for a in range(groups)], axis=1
    )
    return mm(onehot_cols(row & (B - 1), B), spread)


def normalise(first, gain):
    centred = first - jnp.mean(first, axis=-1, keepdims=True)
    inv_std = lax.rsqrt(jnp.mean(centred * centred, axis=-1, keepdims=True) + EPS)
    unit = centred * inv_std
    normed = unit * gain
    bent = jnp.tanh(GELU_SCALE * (normed + GELU_CUBIC * (normed * normed * normed)))
    return unit, inv_std, normed, bent


def gather_step(
    map_ref, before_ref, after_ref, weight_ref, out_ref, table_ref, slots, chans, keep_ref=None
):
    step = pl.program_id(0)
    unroll = weight_ref.shape[0]
    weight = weight_ref[...].reshape(unroll * chans, chans)
    for start in range(0, slots, WIDE):
        size = min(WIDE, slots - start)
        found = []
        for u in range(unroll):
            entry = lane_replicated(map_ref[pl.ds(step * unroll + u, 1), start : start + size])
            rows = pick(entry - F, table_ref, chans)
            parts = []
            for side, face_ref in enumerate((before_ref, after_ref)):
                at = side * F - start
                if 0 <= at < size:
                    near = entry[at : at + F]
                    crossing = mm(onehot_rows(near & (F - 1), F), face_ref[...])
                    parts.append(
                        jnp.where(side_mask(near, side, slots), crossing, rows[at : at + F])
                    )
            if parts:
                parts.append(rows[len(parts) * F :])
                rows = jnp.concatenate(parts, axis=0)
            found.append(rows.astype(jnp.bfloat16))
            if keep_ref is not None:
                keep_ref[u, start : start + size, :] = found[-1]
        out_ref[start : start + size, :] += mm(jnp.concatenate(found, axis=1), weight)


def first_layer_body(
    count_ref, map_ref, field_ref, before_ref, after_ref, weight_ref, gain_ref,
    first_ref, hidden_ref, rows_ref, table_ref,
):
    slots, chans = field_ref.shape
    step = pl.program_id(0)

    @pl.when(step == 0)
    def _():
        first_ref[...] = jnp.zeros_like(first_ref)
        for start in range(0, slots, B):
            field = field_ref[start : start + B, :].astype(jnp.float32)
            field = (field * alive(start, B, count_ref[0], chans)).astype(jnp.bfloat16)
            load_table(table_ref, field, start, B, chans)

    gather_step(
        map_ref, before_ref, after_ref, weight_ref, first_ref, table_ref, slots, chans, rows_ref
    )

    @pl.when(step == pl.num_programs(0) - 1)
    def _():
        for start in range(0, slots, B):
            at = slice(start, start + B)
            _, _, normed, bent = normalise(first_ref[at, :], gain_ref[...])
            act = 0.5 * normed * (1.0 + bent)
            hidden_ref[at, :] = (act * alive(start, B, count_ref[0], chans)).astype(jnp.bfloat16)


def second_layer_body(
    count_ref, map_ref, order_ref, skip_ref, field_ref, below_ref, above_ref, weight_ref,
    serial_ref, second_ref, table_ref,
):
    slots, chans = field_ref.shape
    step = pl.program_id(0)

    @pl.when(step == 0)
    def _():
        second_ref[...] = jnp.zeros_like(second_ref)
        load_table(table_ref, field_ref, 0, slots, chans)

    faces = (below_ref.at[pl.ds(F, F), :], above_ref.at[pl.ds(F, F), :])
    gather_step(map_ref, *faces, weight_ref, second_ref, table_ref, slots, chans)

    @pl.when(step == pl.num_programs(0) - 1)
    def _():
        for start in range(0, slots, B):
            at = slice(start, start + B)
            live = alive(start, B, count_ref[0], chans)
            masked = skip_ref[at, :].astype(jnp.float32) * live
            block = ((masked + second_ref[at, :]) * live).astype(jnp.bfloat16)
            load_table(table_ref, block, start, B, chans)
        for start in range(0, slots, WIDE):
            size = min(WIDE, slots - start)
            index = lane_replicated(order_ref[:, start : start + size])
            serial_ref[start : start + size, :] = pick(index, table_ref, chans).astype(
                jnp.bfloat16
            )


def edge_step(map_ref, weight_ref, grad_ref, edge_ref, near_ref=None):
    chans = grad_ref.shape[1]
    slots = grad_ref.shape[0]
    step = pl.program_id(0)
    unroll = weight_ref.shape[0]
    back = jnp.concatenate([weight_ref[u] for u in range(unroll)], axis=1)
    for side in range(2):
        at = slice(side * F, (side + 1) * F)
        grad = grad_ref[at, :].astype(jnp.float32)
        sums = []
        for u in range(unroll):
            row = map_ref[pl.ds(step * unroll + u, 1), at]
            crossing = jnp.where(side_mask(lane_replicated(row), side, slots), grad, 0.0)
            sums.append(
                mm(onehot_cols(row & (F - 1), F), crossing.astype(jnp.bfloat16)).astype(
                    jnp.bfloat16
                )
            )
            if near_ref is not None:
                near_ref[u, at, :] = sums[-1]
        edge_ref[at, :] += lax.dot_general(
            jnp.concatenate(sums, axis=1), back, NT, preferred_element_type=jnp.float32
        )


def scatter_step(map_ref, weight_ref, grad_ref, total_ref, turned_ref=None, wgrad_ref=None):
    slots, chans = grad_ref.shape
    groups = slots // B
    step = pl.program_id(0)
    unroll = weight_ref.shape[0]
    own = []
    for u in range(unroll):
        row = map_ref[pl.ds(step * unroll + u, 1), :]
        grad = grad_ref[...].astype(jnp.float32)
        own.append(drop(row - F, lane_replicated(row) - F, grad, groups).astype(jnp.bfloat16))
    back = jnp.concatenate([weight_ref[u] for u in range(unroll)], axis=1)
    wide = None
    for a in range(groups):
        piece = jnp.concatenate(
            [own[u][:, a * chans : (a + 1) * chans] for u in range(unroll)], axis=1
        )
        at = slice(a * B, (a + 1) * B)
        total_ref[at, :] += lax.dot_general(piece, back, NT, preferred_element_type=jnp.float32)
        if wgrad_ref is not None:
            term = mm(turned_ref[:, at], piece)
            wide = term if wide is None else wide + term
    if wgrad_ref is not None:
        for u in range(unroll):
            wgrad_ref[u] = wide[:, u * chans : (u + 1) * chans]


def second_edges_body(
    count_ref, map_ref, order_ref, slotted_ref, ends_ref, weight_ref,
    grad_ref, near_ref, up_ref, down_ref, edge_ref,
):
    slots, chans = slotted_ref.shape
    step = pl.program_id(0)

    @pl.when(step == 0)
    def _():
        edge_ref[...] = jnp.zeros_like(edge_ref)
        order = order_ref[...]
        placed = drop(
            order, lane_replicated(order), slotted_ref[...].astype(jnp.float32), slots // B
        )
        for a in range(slots // B):
            live = alive(a * B, B, count_ref[0], chans)
            grad_ref[a * B : (a + 1) * B, :] = (
                placed[:, a * chans : (a + 1) * chans] * live
            ).astype(jnp.bfloat16)

    edge_step(map_ref, weight_ref, grad_ref, edge_ref, near_ref)

    @pl.when(step == pl.num_programs(0) - 1)
    def _():
        up_ref[:F, :] = edge_ref[F:, :].astype(jnp.bfloat16)
        up_ref[F:, :] = ends_ref[F:, :]
        down_ref[:F, :] = edge_ref[:F, :].astype(jnp.bfloat16)
        down_ref[F:, :] = ends_ref[:F, :]


def second_back_body(
    count_ref, map_ref, grad_ref, field_ref, weight_ref, total_ref, wgrad_ref, turned_ref
):
    step = pl.program_id(0)

    @pl.when(step == 0)
    def _():
        total_ref[...] = jnp.zeros_like(total_ref)
        turned_ref[...] = field_ref[...].T

    scatter_step(map_ref, weight_ref, grad_ref, total_ref, turned_ref, wgrad_ref)


def weights_body(
    count_ref, map_ref, first_ref, upper_ref, below_ref, above_ref, gain_ref,
    weight_ref, rows_ref, near_ref, partial_ref,
    grad_ref, wgrad_ref, up_ref, down_ref, turned_ref, faces_ref, edge_ref,
):
    slots, chans = first_ref.shape
    step = pl.program_id(0)
    unroll = rows_ref.shape[0]
    half = wgrad_ref.shape[0] // 2

    @pl.when(step == 0)
    def _():
        edge_ref[...] = jnp.zeros_like(edge_ref)
        gain_term = jnp.zeros((1, chans), jnp.float32)
        faces_ref[:, :F] = below_ref[F:, :].T
        faces_ref[:, F:] = above_ref[F:, :].T
        for start in range(0, slots, B):
            at = slice(start, start + B)
            live = alive(start, B, count_ref[0], chans)
            upper = upper_ref[at, :]
            if start == 0:
                upper = upper + below_ref[:F, :].astype(jnp.float32)
            if start == F:
                upper = upper + above_ref[:F, :].astype(jnp.float32)
            unit, inv_std, normed, bent = normalise(first_ref[at, :], gain_ref[...])
            inner = GELU_SCALE * (1.0 + 3.0 * GELU_CUBIC * (normed * normed))
            slope = 0.5 * (1.0 + bent) + 0.5 * normed * (1.0 - bent * bent) * inner
            grad_normed = slope * (upper * live)
            gain_term = gain_term + jnp.sum(grad_normed * unit, axis=0, keepdims=True)
            grad_unit = grad_normed * gain_ref[...]
            centred = (
                grad_unit
                - jnp.mean(grad_unit, axis=-1, keepdims=True)
                - unit * jnp.mean(grad_unit * unit, axis=-1, keepdims=True)
            )
            grad = (inv_std * centred).astype(jnp.bfloat16)
            grad_ref[at, :] = grad
            turned_ref[:, at] = grad.T
        row = lax.broadcasted_iota(jnp.int32, (chans, chans), 0)
        high = gain_term.astype(jnp.bfloat16).astype(jnp.float32)
        wgrad_ref[half - 1] = jnp.where(
            row == 0, high, jnp.where(row == 1, gain_term - high, 0.0)
        ).astype(jnp.bfloat16)
        wgrad_ref[2 * half - 1] = jnp.zeros((chans, chans), jnp.bfloat16)

    edge_step(map_ref, weight_ref, grad_ref, edge_ref)
    wide = mm(turned_ref[...], jnp.concatenate([rows_ref[u] for u in range(unroll)], axis=1))
    edge = mm(faces_ref[...], jnp.concatenate([near_ref[u] for u in range(unroll)], axis=1))
    for u in range(unroll):
        at = slice(u * chans, (u + 1) * chans)
        wgrad_ref[step * unroll + u] = wide[:, at].T.astype(jnp.bfloat16)
        wgrad_ref[half + step * unroll + u] = (partial_ref[u] + edge[:, at]).astype(jnp.bfloat16)

    @pl.when(step == pl.num_programs(0) - 1)
    def _():
        up_ref[...] = edge_ref[F:, :].astype(jnp.bfloat16)
        down_ref[...] = edge_ref[:F, :].astype(jnp.bfloat16)


def first_back_body(
    count_ref, map_ref, grad_ref, top_ref, from_prev_ref, from_next_ref, weight_ref,
    out_ref, total_ref,
):
    slots, chans = grad_ref.shape
    step = pl.program_id(0)

    @pl.when(step == 0)
    def _():
        total_ref[...] = top_ref[...].astype(jnp.float32)
        total_ref[:F, :] += from_prev_ref[...].astype(jnp.float32)
        total_ref[F : 2 * F, :] += from_next_ref[...].astype(jnp.float32)

    scatter_step(map_ref, weight_ref, grad_ref, total_ref)

    @pl.when(step == pl.num_programs(0) - 1)
    def _():
        live = alive(0, slots, count_ref[0], chans)
        out_ref[...] = (total_ref[...] * live).astype(jnp.bfloat16)


def call(body, name, operands, stepped, outputs, scratch, together=3, dense=True):
    offsets = operands[stepped[0]].shape[0]
    unroll = together if offsets % together == 0 else 1
    slots, chans = operands[1].shape[1], operands[stepped[0]].shape[2]
    width = slots if dense else 4 * chans

    def spec(shape, cut):
        if cut:
            return pl.BlockSpec((unroll,) + shape[1:], lambda k: (k,) + (0,) * (len(shape) - 1))
        return pl.BlockSpec(shape, lambda k: (0,) * len(shape))

    specs = [pl.BlockSpec(memory_space=pltpu.SMEM)]
    specs += [spec(o.shape, n in stepped) for n, o in enumerate(operands) if n > 0]
    return pl.pallas_call(
        body,
        grid=(offsets // unroll,),
        in_specs=specs,
        out_specs=[spec(out[0], len(out) > 2) for out in outputs],
        out_shape=[jax.ShapeDtypeStruct(out[0], out[1]) for out in outputs],
        scratch_shapes=[pltpu.VMEM(shape, dtype) for shape, dtype in scratch],
        compiler_params=PARAMS,
        cost_estimate=pl.CostEstimate(
            flops=7 * offsets * slots * width * chans // 2,
            transcendentals=0,
            bytes_accessed=4 * slots * chans,
        ),
        name=name,
    )(*operands)


def swap_rows(rows):
    return lax.all_to_all(rows, AXES, split_axis=0, concat_axis=0, tiled=True)


def local(
    features, kernel_map, send_order, counts, first_weight, second_weight, norm_gain, cotangent
):
    slots, chans = features.shape
    neighbours = kernel_map[0]
    offsets = neighbours.shape[0]
    devices = lax.axis_size(AXES)
    gain = norm_gain[None, :]
    bf16, f32 = jnp.bfloat16, jnp.float32
    rows16, rows32 = ((slots, chans), bf16), ((slots, chans), f32)
    face16 = ((F, chans), bf16)
    table16 = ((B, slots // B * chans), bf16)
    turned16 = ((chans, slots), bf16)

    ends = jnp.arange(2 * F, dtype=jnp.int32)[:, None] < counts[0]
    ends_x = (features[: 2 * F].astype(f32) * ends.astype(f32)).astype(bf16)
    before_x, after_x = shifted(ends_x[F:], 1), shifted(ends_x[:F], -1)
    slotted = swap_rows(cotangent)
    first, hidden, rows_x = call(
        first_layer_body, "first_layer",
        (counts, neighbours, features, before_x, after_x, first_weight, gain), (5,),
        (rows32, rows16, ((offsets, slots, chans), bf16, True)), (table16,),
    )
    edge32 = ((2 * F, chans), f32)
    ends16 = ((2 * F, chans), bf16)
    grad_live, near, upper_up, upper_down = call(
        second_edges_body, "second_edges",
        (counts, neighbours, send_order, slotted, hidden[: 2 * F], second_weight), (5,),
        (rows16, ((offsets, 2 * F, chans), bf16, True), ends16, ends16), (edge32,), 9, False,
    )
    below, above = shifted(upper_up, 1), shifted(upper_down, -1)
    upper, partial = call(
        second_back_body, "second_back",
        (counts, neighbours, grad_live, hidden, second_weight), (4,),
        (rows32, ((offsets, chans, chans), f32, True)), (turned16,),
    )
    grad_first, wgrads, lower_up, lower_down = call(
        weights_body, "weights",
        (counts, neighbours, first, upper, below, above, gain, first_weight, rows_x, near,
         partial), (7, 8, 9, 10),
        (rows16, ((2 * (offsets + 1), chans, chans), bf16), face16, face16),
        (turned16, ((chans, 2 * F), bf16), edge32), 3, False,
    )
    from_prev, from_next = shifted(lower_up, 1), shifted(lower_down, -1)
    parts = swap_rows(wgrads.reshape(devices, -1, chans))
    hidden, grad_first = lax.optimization_barrier((hidden, grad_first))
    (ordered,) = call(
        second_layer_body, "second_layer",
        (counts, neighbours, send_order, features, hidden, below, above, second_weight),
        (7,), (rows16,), (rows32, table16),
    )
    part = jnp.sum(parts.astype(f32), axis=0).astype(bf16)
    ordered, part, grad_first = lax.optimization_barrier((ordered, part, grad_first))
    per_peer = slots // devices
    both = swap_rows(
        jnp.concatenate(
            [
                ordered.reshape(devices, per_peer, chans),
                jnp.broadcast_to(part[None], (devices,) + part.shape),
            ],
            axis=1,
        )
    )
    serial_out = both[:, :per_peer].reshape(slots, chans)
    shared = both[:, per_peer:]
    (grad_features,) = call(
        first_back_body, "first_back",
        (counts, neighbours, grad_first, grad_live, from_prev, from_next, first_weight), (6,),
        (rows16,), (rows32,),
    )
    shared = shared.reshape(2, offsets + 1, chans, chans)
    first_grad, second_grad = shared[0, :offsets].astype(f32), shared[1, :offsets].astype(f32)
    gain_grad = shared[0, offsets, 0].astype(f32) + shared[0, offsets, 1].astype(f32)
    return (serial_out, grad_features, first_grad, second_grad, gain_grad)


def solution(mesh):
    placed = (
        P(AXES, None),
        P(AXES, None, None),
        P(AXES, None),
        P(AXES),
        P(),
        P(),
        P(),
        P(AXES, None),
    )
    return jax.shard_map(
        local,
        mesh=mesh,
        in_specs=placed,
        out_specs=(P(AXES, None), P(AXES, None), P(), P(), P()),
        check_vma=False,
    )
```

```python
import jax
import jax.numpy as jnp
from jax import lax
from jax.experimental import pallas as pl
from jax.experimental.pallas import tpu as pltpu
from jax.sharding import PartitionSpec as P

F = 256
B = 256
SHIFT = 8
WIDE = 1024
EPS = 1e-05
GELU_SCALE = 0.7978845608028654
GELU_CUBIC = 0.044715
AXES = ("group", "tile")
NT = (((1,), (1,)), ((), ()))
PARAMS = pltpu.CompilerParams(
    dimension_semantics=("arbitrary",), vmem_limit_bytes=58 * 1024 * 1024
)


def shifted(value, steps):
    count = lax.axis_size(AXES)
    initial, last = (max(0, -steps), min(count, count - steps))
    return lax.ppermute(value, AXES, [(source, source + steps) for source in range(initial, last)])


def mm(a, b):
    return jnp.dot(a, b, preferred_element_type=jnp.float32)


def lane_replicated(row):
    parts = [
        jnp.broadcast_to(row[:, j : j + 128], (128, 128)).T for j in range(0, row.shape[1], 128)
    ]
    return jnp.concatenate(parts, axis=0)


def onehot_rows(index, width):
    lanes = lax.broadcasted_iota(jnp.int32, index.shape, 1)
    parts = [
        jnp.where(index == lanes + j, 1.0, 0.0).astype(jnp.bfloat16) for j in range(0, width, 128)
    ]
    return jnp.concatenate(parts, axis=1)


def onehot_cols(row, height):
    shape = (height, row.shape[1])
    return jnp.where(
        jnp.broadcast_to(row, shape) == lax.broadcasted_iota(jnp.int32, shape, 0), 1.0, 0.0
    ).astype(jnp.bfloat16)


def side_mask(entry, side, slots):
    if side == 0:
        return entry < F
    return (entry >= slots + F) & (entry < slots + 2 * F)


def alive(start, size, count, chans):
    rows = lax.broadcasted_iota(jnp.int32, (size, chans), 0) + start
    return jnp.where(rows < count, 1.0, 0.0)


def load_table(table_ref, field, start, size, chans):
    for a in range(start // B, (start + size) // B):
        at = a * B - start
        table_ref[:, a * chans : (a + 1) * chans] = field[at : at + B]


def pick(index, table_ref, chans):
    picked = mm(onehot_rows(index & (B - 1), B), table_ref[...])
    high = index >> SHIFT
    rows = jnp.where(high == 0, picked[:, :chans], 0.0)
    for a in range(1, table_ref.shape[1] // chans):
        rows = jnp.where(high == a, picked[:, a * chans : (a + 1) * chans], rows)
    return rows


def drop(row, index, value, groups):
    high = index >> SHIFT
    spread = jnp.concatenate(
        [jnp.where(high == a, value, 0.0).astype(jnp.bfloat16) for a in range(groups)], axis=1
    )
    return mm(onehot_cols(row & (B - 1), B), spread)


def normalise(first, gain):
    centred = first - jnp.mean(first, axis=-1, keepdims=True)
    inv_std = lax.rsqrt(jnp.mean(centred * centred, axis=-1, keepdims=True) + EPS)
    unit = centred * inv_std
    normed = unit * gain
    bent = jnp.tanh(GELU_SCALE * (normed + GELU_CUBIC * (normed * normed * normed)))
    return unit, inv_std, normed, bent


def map_row(map_ref, nth):
    return pl.ds(nth + (nth >= map_ref.shape[0] // 2).astype(jnp.int32), 1)


def gather_step(
    map_ref, before_ref, after_ref, weight_refs, out_ref, table_ref, slots, chans, keep_ref=None
):
    step = pl.program_id(0)
    unroll = len(weight_refs)
    weight = jnp.concatenate([ref[0] for ref in weight_refs], axis=0)
    for start in range(0, slots, WIDE):
        size = min(WIDE, slots - start)
        found = []
        for u in range(unroll):
            row = map_ref[map_row(map_ref, step * unroll + u), start : start + size]
            entry = lane_replicated(row)
            rows = pick(entry - F, table_ref, chans)
            parts = []
            for side, face_ref in enumerate((before_ref, after_ref)):
                at = side * F - start
                if 0 <= at < size:
                    near = entry[at : at + F]
                    crossing = mm(onehot_rows(near & (F - 1), F), face_ref[...])
                    parts.append(
                        jnp.where(side_mask(near, side, slots), crossing, rows[at : at + F])
                    )
            if parts:
                parts.append(rows[len(parts) * F :])
                rows = jnp.concatenate(parts, axis=0)
            found.append(rows.astype(jnp.bfloat16))
            if keep_ref is not None:
                keep_ref[u, start : start + size, :] = found[-1]
        out_ref[start : start + size, :] += mm(jnp.concatenate(found, axis=1), weight)


def first_layer_body(
    count_ref, map_ref, field_ref, before_ref, after_ref, gain_ref, weight_refs, centre_ref,
    hidden_ref, unit_ref, inv_ref, slope_ref, rows_ref, first_ref, table_ref,
):
    slots, chans = field_ref.shape
    step = pl.program_id(0)

    @pl.when(step == 0)
    def _():
        for start in range(0, slots, B):
            field = field_ref[start : start + B, :].astype(jnp.float32)
            field = (field * alive(start, B, count_ref[0], chans)).astype(jnp.bfloat16)
            load_table(table_ref, field, start, B, chans)
            first_ref[start : start + B, :] = mm(field, centre_ref[0])

    gather_step(
        map_ref, before_ref, after_ref, weight_refs, first_ref, table_ref, slots, chans, rows_ref
    )

    @pl.when(step == pl.num_programs(0) - 1)
    def _():
        for start in range(0, slots, B):
            at = slice(start, start + B)
            unit, inv_std, normed, bent = normalise(first_ref[at, :], gain_ref[...])
            act = 0.5 * normed * (1.0 + bent)
            live = alive(start, B, count_ref[0], chans)
            hidden_ref[at, :] = (act * live).astype(jnp.bfloat16)
            inner = GELU_SCALE * (1.0 + 3.0 * GELU_CUBIC * (normed * normed))
            slope = 0.5 * (1.0 + bent) + 0.5 * normed * (1.0 - bent * bent) * inner
            unit_ref[at, :] = unit
            inv_ref[at, :] = jnp.broadcast_to(inv_std, (B, chans))
            slope_ref[at, :] = slope * live


def second_layer_body(
    count_ref, map_ref, order_ref, skip_ref, field_ref, below_ref, above_ref, weight_refs,
    centre_ref, serial_ref, second_ref, table_ref,
):
    slots, chans = field_ref.shape
    step = pl.program_id(0)

    @pl.when(step == 0)
    def _():
        second_ref[...] = mm(field_ref[...], centre_ref[0])
        load_table(table_ref, field_ref, 0, slots, chans)

    faces = (below_ref.at[pl.ds(F, F), :], above_ref.at[pl.ds(F, F), :])
    gather_step(map_ref, *faces, weight_refs, second_ref, table_ref, slots, chans)

    @pl.when(step == pl.num_programs(0) - 1)
    def _():
        for start in range(0, slots, B):
            at = slice(start, start + B)
            live = alive(start, B, count_ref[0], chans)
            masked = skip_ref[at, :].astype(jnp.float32) * live
            block = ((masked + second_ref[at, :]) * live).astype(jnp.bfloat16)
            load_table(table_ref, block, start, B, chans)
        for start in range(0, slots, WIDE):
            size = min(WIDE, slots - start)
            index = lane_replicated(order_ref[:, start : start + size])
            serial_ref[start : start + size, :] = pick(index, table_ref, chans).astype(
                jnp.bfloat16
            )


def edge_step(map_ref, weight_refs, grad_ref, edge_ref, near_ref=None):
    chans = grad_ref.shape[1]
    slots = grad_ref.shape[0]
    step = pl.program_id(0)
    unroll = len(weight_refs)
    back = jnp.concatenate([ref[0] for ref in weight_refs], axis=1)
    for side in range(2):
        at = slice(side * F, (side + 1) * F)
        grad = grad_ref[at, :].astype(jnp.float32)
        sums = []
        for u in range(unroll):
            row = map_ref[map_row(map_ref, step * unroll + u), at]
            crossing = jnp.where(side_mask(lane_replicated(row), side, slots), grad, 0.0)
            sums.append(
                mm(onehot_cols(row & (F - 1), F), crossing.astype(jnp.bfloat16)).astype(
                    jnp.bfloat16
                )
            )
            if near_ref is not None:
                near_ref[u, at, :] = sums[-1]
        edge_ref[at, :] += lax.dot_general(
            jnp.concatenate(sums, axis=1), back, NT, preferred_element_type=jnp.float32
        )


def scatter_step(map_ref, weight_refs, grad_ref, total_ref, turned_ref=None, wgrad_ref=None):
    slots, chans = grad_ref.shape
    groups = slots // B
    step = pl.program_id(0)
    unroll = len(weight_refs)
    own = []
    for u in range(unroll):
        row = map_ref[map_row(map_ref, step * unroll + u), :]
        grad = grad_ref[...].astype(jnp.float32)
        own.append(drop(row - F, lane_replicated(row) - F, grad, groups).astype(jnp.bfloat16))
    back = jnp.concatenate([ref[0] for ref in weight_refs], axis=1)
    wide = None
    for a in range(groups):
        piece = jnp.concatenate(
            [own[u][:, a * chans : (a + 1) * chans] for u in range(unroll)], axis=1
        )
        at = slice(a * B, (a + 1) * B)
        total_ref[at, :] += lax.dot_general(piece, back, NT, preferred_element_type=jnp.float32)
        if wgrad_ref is not None:
            term = mm(turned_ref[:, at], piece)
            wide = term if wide is None else wide + term
    if wgrad_ref is not None:
        for u in range(unroll):
            wgrad_ref[u] = wide[:, u * chans : (u + 1) * chans]


def second_edges_body(
    count_ref, map_ref, order_ref, slotted_ref, ends_ref, weight_refs, centre_ref,
    grad_ref, near_ref, up_ref, down_ref, edge_ref,
):
    slots, chans = slotted_ref.shape
    step = pl.program_id(0)

    @pl.when(step == 0)
    def _():
        edge_ref[...] = jnp.zeros_like(edge_ref)
        order = order_ref[...]
        placed = drop(
            order, lane_replicated(order), slotted_ref[...].astype(jnp.float32), slots // B
        )
        for a in range(slots // B):
            live = alive(a * B, B, count_ref[0], chans)
            grad_ref[a * B : (a + 1) * B, :] = (
                placed[:, a * chans : (a + 1) * chans] * live
            ).astype(jnp.bfloat16)

    edge_step(map_ref, weight_refs, grad_ref, edge_ref, near_ref)

    @pl.when(step == pl.num_programs(0) - 1)
    def _():
        up_ref[:F, :] = edge_ref[F:, :].astype(jnp.bfloat16)
        up_ref[F:, :] = ends_ref[F:, :]
        down_ref[:F, :] = edge_ref[:F, :].astype(jnp.bfloat16)
        down_ref[F:, :] = ends_ref[:F, :]


def second_back_body(
    count_ref, map_ref, grad_ref, field_ref, weight_refs, centre_ref,
    total_ref, wgrad_ref, middle_ref, turned_ref,
):
    step = pl.program_id(0)

    @pl.when(step == 0)
    def _():
        total_ref[...] = lax.dot_general(
            grad_ref[...], centre_ref[0], NT, preferred_element_type=jnp.float32
        )
        turned_ref[...] = field_ref[...].T
        middle_ref[...] = mm(turned_ref[...], grad_ref[...])

    scatter_step(map_ref, weight_refs, grad_ref, total_ref, turned_ref, wgrad_ref)


def weights_body(
    count_ref, map_ref, unit_ref, inv_ref, slope_ref, upper_ref, below_ref, above_ref, gain_ref,
    field_ref, middle_ref, weight_refs, centre_ref, rows_ref, near_ref, partial_ref,
    grad_ref, wgrad_ref, up_ref, down_ref, turned_ref, faces_ref, edge_ref,
):
    slots, chans = unit_ref.shape
    step = pl.program_id(0)
    unroll = rows_ref.shape[0]
    half = wgrad_ref.shape[0] // 2

    @pl.when(step == 0)
    def _():
        edge_ref[...] = jnp.zeros_like(edge_ref)
        gain_term = jnp.zeros((1, chans), jnp.float32)
        faces_ref[:, :F] = below_ref[F:, :].T
        faces_ref[:, F:] = above_ref[F:, :].T
        for start in range(0, slots, B):
            at = slice(start, start + B)
            live = alive(start, B, count_ref[0], chans)
            upper = upper_ref[at, :]
            if start == 0:
                upper = upper + below_ref[:F, :].astype(jnp.float32)
            if start == F:
                upper = upper + above_ref[:F, :].astype(jnp.float32)
            unit, inv_std = unit_ref[at, :], inv_ref[at, :]
            grad_normed = slope_ref[at, :] * upper
            gain_term = gain_term + jnp.sum(grad_normed * unit, axis=0, keepdims=True)
            grad_unit = grad_normed * gain_ref[...]
            centred = (
                grad_unit
                - jnp.mean(grad_unit, axis=-1, keepdims=True)
                - unit * jnp.mean(grad_unit * unit, axis=-1, keepdims=True)
            )
            grad = (inv_std * centred).astype(jnp.bfloat16)
            grad_ref[at, :] = grad
            turned_ref[:, at] = grad.T
            field = (field_ref[at, :].astype(jnp.float32) * live).astype(jnp.bfloat16)
            term = mm(turned_ref[:, at], field)
            centre_term = term if start == 0 else centre_term + term
        middle = (half - 1) // 2
        wgrad_ref[middle] = centre_term.T.astype(jnp.bfloat16)
        wgrad_ref[half + middle] = middle_ref[...].astype(jnp.bfloat16)
        row = lax.broadcasted_iota(jnp.int32, (chans, chans), 0)
        high = gain_term.astype(jnp.bfloat16).astype(jnp.float32)
        wgrad_ref[half - 1] = jnp.where(
            row == 0, high, jnp.where(row == 1, gain_term - high, 0.0)
        ).astype(jnp.bfloat16)
        wgrad_ref[2 * half - 1] = jnp.zeros((chans, chans), jnp.bfloat16)

    edge_step(map_ref, weight_refs, grad_ref, edge_ref)
    wide = mm(turned_ref[...], jnp.concatenate([rows_ref[u] for u in range(unroll)], axis=1))
    edge = mm(faces_ref[...], jnp.concatenate([near_ref[u] for u in range(unroll)], axis=1))
    for u in range(unroll):
        at = slice(u * chans, (u + 1) * chans)
        nth = step * unroll + u
        nth = nth + (nth >= (half - 1) // 2).astype(jnp.int32)
        wgrad_ref[nth] = wide[:, at].T.astype(jnp.bfloat16)
        wgrad_ref[half + nth] = (partial_ref[u] + edge[:, at]).astype(jnp.bfloat16)

    @pl.when(step == pl.num_programs(0) - 1)
    def _():
        up_ref[...] = edge_ref[F:, :].astype(jnp.bfloat16)
        down_ref[...] = edge_ref[:F, :].astype(jnp.bfloat16)


def first_back_body(
    count_ref, map_ref, grad_ref, top_ref, from_prev_ref, from_next_ref, weight_refs,
    centre_ref, out_ref, total_ref,
):
    slots, chans = grad_ref.shape
    step = pl.program_id(0)

    @pl.when(step == 0)
    def _():
        total_ref[...] = top_ref[...].astype(jnp.float32) + lax.dot_general(
            grad_ref[...], centre_ref[0], NT, preferred_element_type=jnp.float32
        )
        total_ref[:F, :] += from_prev_ref[...].astype(jnp.float32)
        total_ref[F : 2 * F, :] += from_next_ref[...].astype(jnp.float32)

    scatter_step(map_ref, weight_refs, grad_ref, total_ref)

    @pl.when(step == pl.num_programs(0) - 1)
    def _():
        live = alive(0, slots, count_ref[0], chans)
        out_ref[...] = (total_ref[...] * live).astype(jnp.bfloat16)


def call(body, name, operands, weights, stepped, outputs, scratch, together=2, dense=True):
    offsets, slots = operands[1].shape
    chans = weights.shape[2]
    centre = offsets // 2
    count = offsets - 1
    unroll = together if count % together == 0 else 1
    width = slots if dense else 4 * chans

    def whole(shape):
        return pl.BlockSpec(shape, lambda k: (0,) * len(shape))

    def cut(shape):
        return pl.BlockSpec((unroll,) + shape[1:], lambda k: (k,) + (0,) * (len(shape) - 1))

    def nth_weight(u):
        def at(k):
            nth = k * unroll + u
            return (jnp.where(nth >= centre, nth + 1, nth), 0, 0)

        return pl.BlockSpec((1, chans, chans), at)

    split = len(operands)

    def wrapped(*refs):
        after = split + unroll
        body(*refs[:split], refs[split:after], *refs[after:])

    specs = [pl.BlockSpec(memory_space=pltpu.SMEM)]
    specs += [whole(operand.shape) for operand in operands[1:]]
    specs += [nth_weight(u) for u in range(unroll)]
    specs.append(pl.BlockSpec((1, chans, chans), lambda k: (centre, 0, 0)))
    specs += [cut(operand.shape) for operand in stepped]
    return pl.pallas_call(
        wrapped,
        grid=(count // unroll,),
        in_specs=specs,
        out_specs=[cut(out[0]) if len(out) > 2 else whole(out[0]) for out in outputs],
        out_shape=[jax.ShapeDtypeStruct(out[0], out[1]) for out in outputs],
        scratch_shapes=[pltpu.VMEM(shape, dtype) for shape, dtype in scratch],
        compiler_params=PARAMS,
        cost_estimate=pl.CostEstimate(
            flops=7 * offsets * slots * width * chans // 2,
            transcendentals=0,
            bytes_accessed=4 * slots * chans,
        ),
        name=name,
    )(*operands, *([weights] * (unroll + 1)), *stepped)


def swap_rows(rows):
    return lax.all_to_all(rows, AXES, split_axis=0, concat_axis=0, tiled=True)


def local(
    features, kernel_map, send_order, counts, first_weight, second_weight, norm_gain, cotangent
):
    slots, chans = features.shape
    neighbours = kernel_map[0]
    offsets = neighbours.shape[0]
    devices = lax.axis_size(AXES)
    gain = norm_gain[None, :]
    bf16, f32 = jnp.bfloat16, jnp.float32
    rows16, rows32 = ((slots, chans), bf16), ((slots, chans), f32)
    face16 = ((F, chans), bf16)
    table16 = ((B, slots // B * chans), bf16)
    turned16 = ((chans, slots), bf16)

    ends = jnp.arange(2 * F, dtype=jnp.int32)[:, None] < counts[0]
    ends_x = (features[: 2 * F].astype(f32) * ends.astype(f32)).astype(bf16)
    before_x, after_x = shifted(ends_x[F:], 1), shifted(ends_x[:F], -1)
    slotted = swap_rows(cotangent)
    hidden, unit, inv_std, slope, rows_x = call(
        first_layer_body, "first_layer",
        (counts, neighbours, features, before_x, after_x, gain), first_weight, (),
        (rows16, rows32, rows32, rows32, ((offsets - 1, slots, chans), bf16, True)),
        (rows32, table16),
    )
    edge32 = ((2 * F, chans), f32)
    ends16 = ((2 * F, chans), bf16)
    grad_live, near, upper_up, upper_down = call(
        second_edges_body, "second_edges",
        (counts, neighbours, send_order, slotted, hidden[: 2 * F]), second_weight, (),
        (rows16, ((offsets - 1, 2 * F, chans), bf16, True), ends16, ends16), (edge32,), 13, False,
    )
    below, above = shifted(upper_up, 1), shifted(upper_down, -1)
    upper, partial, middle = call(
        second_back_body, "second_back",
        (counts, neighbours, grad_live, hidden), second_weight, (),
        (rows32, ((offsets - 1, chans, chans), f32, True), ((chans, chans), f32)), (turned16,),
    )
    grad_first, wgrads, lower_up, lower_down = call(
        weights_body, "weights",
        (counts, neighbours, unit, inv_std, slope, upper, below, above, gain, features, middle),
        first_weight, (rows_x, near, partial),
        (rows16, ((2 * (offsets + 1), chans, chans), bf16), face16, face16),
        (turned16, ((chans, 2 * F), bf16), edge32), 2, False,
    )
    from_prev, from_next = shifted(lower_up, 1), shifted(lower_down, -1)
    parts = swap_rows(wgrads.reshape(devices, -1, chans))
    hidden, grad_first = lax.optimization_barrier((hidden, grad_first))
    (ordered,) = call(
        second_layer_body, "second_layer",
        (counts, neighbours, send_order, features, hidden, below, above), second_weight,
        (), (rows16,), (rows32, table16),
    )
    part = jnp.sum(parts.astype(f32), axis=0).astype(bf16)
    ordered, part, grad_first = lax.optimization_barrier((ordered, part, grad_first))
    per_peer = slots // devices
    both = swap_rows(
        jnp.concatenate(
            [
                ordered.reshape(devices, per_peer, chans),
                jnp.broadcast_to(part[None], (devices,) + part.shape),
            ],
            axis=1,
        )
    )
    serial_out = both[:, :per_peer].reshape(slots, chans)
    shared = both[:, per_peer:]
    (grad_features,) = call(
        first_back_body, "first_back",
        (counts, neighbours, grad_first, grad_live, from_prev, from_next), first_weight, (),
        (rows16,), (rows32,),
    )
    shared = shared.reshape(2, offsets + 1, chans, chans)
    first_grad, second_grad = shared[0, :offsets].astype(f32), shared[1, :offsets].astype(f32)
    gain_grad = shared[0, offsets, 0].astype(f32) + shared[0, offsets, 1].astype(f32)
    return (serial_out, grad_features, first_grad, second_grad, gain_grad)


def solution(mesh):
    placed = (
        P(AXES, None),
        P(AXES, None, None),
        P(AXES, None),
        P(AXES),
        P(),
        P(),
        P(),
        P(AXES, None),
    )
    return jax.shard_map(
        local,
        mesh=mesh,
        in_specs=placed,
        out_specs=(P(AXES, None), P(AXES, None), P(), P(), P()),
        check_vma=False,
    )
```

```python
import jax
import jax.numpy as jnp
from jax import lax
from jax.experimental import pallas as pl
from jax.experimental.pallas import tpu as pltpu
from jax.sharding import PartitionSpec as P

F = 256
B = 256
SHIFT = 8
TABLE = 512
TABLE_SHIFT = 9
TOGETHER = 3
TOGETHER_SCATTER = 9
TOGETHER_WEIGHTS = 9
TOGETHER_EDGES = 27
WIDE = 1024
EPS = 1e-05
GELU_SCALE = 0.7978845608028654
GELU_CUBIC = 0.044715
AXES = ("group", "tile")
NT = (((1,), (1,)), ((), ()))
PARAMS = pltpu.CompilerParams(
    dimension_semantics=("arbitrary",), vmem_limit_bytes=58 * 1024 * 1024
)


def shifted(value, steps):
    count = lax.axis_size(AXES)
    initial, last = (max(0, -steps), min(count, count - steps))
    return lax.ppermute(value, AXES, [(source, source + steps) for source in range(initial, last)])


def mm(a, b):
    return jnp.dot(a, b, preferred_element_type=jnp.float32)


def lane_replicated(row):
    parts = [
        jnp.broadcast_to(row[:, j : j + 128], (128, 128)).T for j in range(0, row.shape[1], 128)
    ]
    return jnp.concatenate(parts, axis=0)


def onehot_rows(index, width):
    lanes = lax.broadcasted_iota(jnp.int32, index.shape, 1)
    parts = [
        jnp.where(index == lanes + j, 1.0, 0.0).astype(jnp.bfloat16) for j in range(0, width, 128)
    ]
    return jnp.concatenate(parts, axis=1)


def onehot_cols(row, height):
    shape = (height, row.shape[1])
    return jnp.where(
        jnp.broadcast_to(row, shape) == lax.broadcasted_iota(jnp.int32, shape, 0), 1.0, 0.0
    ).astype(jnp.bfloat16)


def side_mask(entry, side, slots):
    if side == 0:
        return entry < F
    return (entry >= slots + F) & (entry < slots + 2 * F)


def alive(start, size, count, chans):
    rows = lax.broadcasted_iota(jnp.int32, (size, chans), 0) + start
    return jnp.where(rows < count, 1.0, 0.0)


def load_table(table_ref, field, start, size, chans):
    for a in range(start // TABLE, (start + size) // TABLE):
        at = a * TABLE - start
        table_ref[:, a * chans : (a + 1) * chans] = field[at : at + TABLE]


def pick(index, table_ref, chans):
    picked = mm(onehot_rows(index & (TABLE - 1), TABLE), table_ref[...])
    high = index >> TABLE_SHIFT
    rows = jnp.where(high == 0, picked[:, :chans], 0.0)
    for a in range(1, table_ref.shape[1] // chans):
        rows = jnp.where(high == a, picked[:, a * chans : (a + 1) * chans], rows)
    return rows


def drop(row, index, value, groups):
    high = index >> SHIFT
    spread = jnp.concatenate(
        [jnp.where(high == a, value, 0.0).astype(jnp.bfloat16) for a in range(groups)], axis=1
    )
    return mm(onehot_cols(row & (B - 1), B), spread)


def normalise(first, gain):
    centred = first - jnp.mean(first, axis=-1, keepdims=True)
    inv_std = lax.rsqrt(jnp.mean(centred * centred, axis=-1, keepdims=True) + EPS)
    unit = centred * inv_std
    normed = unit * gain
    bent = jnp.tanh(GELU_SCALE * (normed + GELU_CUBIC * (normed * normed * normed)))
    return unit, inv_std, normed, bent


def gather_step(
    map_ref, before_ref, after_ref, weight_ref, out_ref, table_ref, slots, chans, keep_ref=None
):
    step = pl.program_id(0)
    unroll = weight_ref.shape[0]
    weight = weight_ref[...].reshape(unroll * chans, chans)
    for start in range(0, slots, WIDE):
        size = min(WIDE, slots - start)
        found = []
        for u in range(unroll):
            entry = lane_replicated(map_ref[pl.ds(step * unroll + u, 1), start : start + size])
            rows = pick(entry - F, table_ref, chans)
            parts = []
            for side, face_ref in enumerate((before_ref, after_ref)):
                at = side * F - start
                if 0 <= at < size:
                    near = entry[at : at + F]
                    crossing = mm(onehot_rows(near & (F - 1), F), face_ref[...])
                    parts.append(
                        jnp.where(side_mask(near, side, slots), crossing, rows[at : at + F])
                    )
            if parts:
                parts.append(rows[len(parts) * F :])
                rows = jnp.concatenate(parts, axis=0)
            found.append(rows.astype(jnp.bfloat16))
            if keep_ref is not None:
                keep_ref[u, start : start + size, :] = found[-1]
        out_ref[start : start + size, :] += mm(jnp.concatenate(found, axis=1), weight)


def first_layer_body(
    count_ref, map_ref, field_ref, before_ref, after_ref, weight_ref, gain_ref,
    first_ref, hidden_ref, rows_ref, table_ref,
):
    slots, chans = field_ref.shape
    step = pl.program_id(0)

    @pl.when(step == 0)
    def _():
        first_ref[...] = jnp.zeros_like(first_ref)
        for start in range(0, slots, TABLE):
            field = field_ref[start : start + TABLE, :].astype(jnp.float32)
            field = (field * alive(start, TABLE, count_ref[0], chans)).astype(jnp.bfloat16)
            load_table(table_ref, field, start, TABLE, chans)

    gather_step(
        map_ref, before_ref, after_ref, weight_ref, first_ref, table_ref, slots, chans, rows_ref
    )

    @pl.when(step == pl.num_programs(0) - 1)
    def _():
        for start in range(0, slots, B):
            at = slice(start, start + B)
            _, _, normed, bent = normalise(first_ref[at, :], gain_ref[...])
            act = 0.5 * normed * (1.0 + bent)
            hidden_ref[at, :] = (act * alive(start, B, count_ref[0], chans)).astype(jnp.bfloat16)


def second_layer_body(
    count_ref, map_ref, order_ref, skip_ref, field_ref, below_ref, above_ref, weight_ref,
    serial_ref, second_ref, table_ref,
):
    slots, chans = field_ref.shape
    step = pl.program_id(0)

    @pl.when(step == 0)
    def _():
        second_ref[...] = jnp.zeros_like(second_ref)
        load_table(table_ref, field_ref, 0, slots, chans)

    faces = (below_ref.at[pl.ds(F, F), :], above_ref.at[pl.ds(F, F), :])
    gather_step(map_ref, *faces, weight_ref, second_ref, table_ref, slots, chans)

    @pl.when(step == pl.num_programs(0) - 1)
    def _():
        for start in range(0, slots, TABLE):
            at = slice(start, start + TABLE)
            live = alive(start, TABLE, count_ref[0], chans)
            masked = skip_ref[at, :].astype(jnp.float32) * live
            block = ((masked + second_ref[at, :]) * live).astype(jnp.bfloat16)
            load_table(table_ref, block, start, TABLE, chans)
        for start in range(0, slots, WIDE):
            size = min(WIDE, slots - start)
            index = lane_replicated(order_ref[:, start : start + size])
            serial_ref[start : start + size, :] = pick(index, table_ref, chans).astype(
                jnp.bfloat16
            )


def edge_step(map_ref, weight_ref, grad_ref, edge_ref, near_ref=None):
    chans = grad_ref.shape[1]
    slots = grad_ref.shape[0]
    step = pl.program_id(0)
    unroll = weight_ref.shape[0]
    back = jnp.concatenate([weight_ref[u] for u in range(unroll)], axis=1)
    for side in range(2):
        at = slice(side * F, (side + 1) * F)
        grad = grad_ref[at, :].astype(jnp.float32)
        sums = []
        for u in range(unroll):
            row = map_ref[pl.ds(step * unroll + u, 1), at]
            crossing = jnp.where(side_mask(lane_replicated(row), side, slots), grad, 0.0)
            sums.append(
                mm(onehot_cols(row & (F - 1), F), crossing.astype(jnp.bfloat16)).astype(
                    jnp.bfloat16
                )
            )
            if near_ref is not None:
                near_ref[u, at, :] = sums[-1]
        edge_ref[at, :] += lax.dot_general(
            jnp.concatenate(sums, axis=1), back, NT, preferred_element_type=jnp.float32
        )


def scatter_step(map_ref, weight_ref, grad_ref, total_ref, turned_ref=None, wgrad_ref=None):
    slots, chans = grad_ref.shape
    groups = slots // B
    step = pl.program_id(0)
    unroll = weight_ref.shape[0]
    own = []
    for u in range(unroll):
        row = map_ref[pl.ds(step * unroll + u, 1), :]
        grad = grad_ref[...].astype(jnp.float32)
        own.append(drop(row - F, lane_replicated(row) - F, grad, groups).astype(jnp.bfloat16))
    back = jnp.concatenate([weight_ref[u] for u in range(unroll)], axis=1)
    wide = None
    for a in range(groups):
        piece = jnp.concatenate(
            [own[u][:, a * chans : (a + 1) * chans] for u in range(unroll)], axis=1
        )
        at = slice(a * B, (a + 1) * B)
        total_ref[at, :] += lax.dot_general(piece, back, NT, preferred_element_type=jnp.float32)
        if wgrad_ref is not None:
            term = mm(turned_ref[:, at], piece)
            wide = term if wide is None else wide + term
    if wgrad_ref is not None:
        for u in range(unroll):
            wgrad_ref[u] = wide[:, u * chans : (u + 1) * chans]


def second_edges_body(
    count_ref, map_ref, order_ref, slotted_ref, ends_ref, weight_ref,
    grad_ref, near_ref, up_ref, down_ref, edge_ref,
):
    slots, chans = slotted_ref.shape
    step = pl.program_id(0)

    @pl.when(step == 0)
    def _():
        edge_ref[...] = jnp.zeros_like(edge_ref)
        order = order_ref[...]
        placed = drop(
            order, lane_replicated(order), slotted_ref[...].astype(jnp.float32), slots // B
        )
        for a in range(slots // B):
            live = alive(a * B, B, count_ref[0], chans)
            grad_ref[a * B : (a + 1) * B, :] = (
                placed[:, a * chans : (a + 1) * chans] * live
            ).astype(jnp.bfloat16)

    edge_step(map_ref, weight_ref, grad_ref, edge_ref, near_ref)

    @pl.when(step == pl.num_programs(0) - 1)
    def _():
        up_ref[:F, :] = edge_ref[F:, :].astype(jnp.bfloat16)
        up_ref[F:, :] = ends_ref[F : 2 * F, :]
        down_ref[:F, :] = edge_ref[:F, :].astype(jnp.bfloat16)
        down_ref[F:, :] = ends_ref[:F, :]


def second_back_body(
    count_ref, map_ref, grad_ref, field_ref, weight_ref, total_ref, wgrad_ref, turned_ref
):
    step = pl.program_id(0)

    @pl.when(step == 0)
    def _():
        total_ref[...] = jnp.zeros_like(total_ref)
        turned_ref[...] = field_ref[...].T

    scatter_step(map_ref, weight_ref, grad_ref, total_ref, turned_ref, wgrad_ref)


def weights_body(
    count_ref, map_ref, first_ref, upper_ref, below_ref, above_ref, gain_ref,
    weight_ref, rows_ref, near_ref, partial_ref,
    grad_ref, wgrad_ref, up_ref, down_ref, turned_ref, faces_ref, edge_ref,
):
    slots, chans = first_ref.shape
    step = pl.program_id(0)
    unroll = rows_ref.shape[0]
    half = wgrad_ref.shape[0] // 2

    @pl.when(step == 0)
    def _():
        edge_ref[...] = jnp.zeros_like(edge_ref)
        gain_term = jnp.zeros((1, chans), jnp.float32)
        faces_ref[:, :F] = below_ref[F:, :].T
        faces_ref[:, F:] = above_ref[F:, :].T
        for start in range(0, slots, B):
            at = slice(start, start + B)
            live = alive(start, B, count_ref[0], chans)
            upper = upper_ref[at, :]
            if start == 0:
                upper = upper + below_ref[:F, :].astype(jnp.float32)
            if start == F:
                upper = upper + above_ref[:F, :].astype(jnp.float32)
            unit, inv_std, normed, bent = normalise(first_ref[at, :], gain_ref[...])
            inner = GELU_SCALE * (1.0 + 3.0 * GELU_CUBIC * (normed * normed))
            slope = 0.5 * (1.0 + bent) + 0.5 * normed * (1.0 - bent * bent) * inner
            grad_normed = slope * (upper * live)
            gain_term = gain_term + jnp.sum(grad_normed * unit, axis=0, keepdims=True)
            grad_unit = grad_normed * gain_ref[...]
            centred = (
                grad_unit
                - jnp.mean(grad_unit, axis=-1, keepdims=True)
                - unit * jnp.mean(grad_unit * unit, axis=-1, keepdims=True)
            )
            grad = (inv_std * centred).astype(jnp.bfloat16)
            grad_ref[at, :] = grad
            turned_ref[:, at] = grad.T
        row = lax.broadcasted_iota(jnp.int32, (chans, chans), 0)
        high = gain_term.astype(jnp.bfloat16).astype(jnp.float32)
        wgrad_ref[half - 1] = jnp.where(
            row == 0, high, jnp.where(row == 1, gain_term - high, 0.0)
        ).astype(jnp.bfloat16)
        wgrad_ref[2 * half - 1] = jnp.zeros((chans, chans), jnp.bfloat16)

    edge_step(map_ref, weight_ref, grad_ref, edge_ref)
    wide = mm(turned_ref[...], jnp.concatenate([rows_ref[u] for u in range(unroll)], axis=1))
    edge = mm(faces_ref[...], jnp.concatenate([near_ref[u] for u in range(unroll)], axis=1))
    for u in range(unroll):
        at = slice(u * chans, (u + 1) * chans)
        wgrad_ref[step * unroll + u] = wide[:, at].T.astype(jnp.bfloat16)
        wgrad_ref[half + step * unroll + u] = (partial_ref[u] + edge[:, at]).astype(jnp.bfloat16)

    @pl.when(step == pl.num_programs(0) - 1)
    def _():
        up_ref[...] = edge_ref[F:, :].astype(jnp.bfloat16)
        down_ref[...] = edge_ref[:F, :].astype(jnp.bfloat16)


def first_back_body(
    count_ref, map_ref, grad_ref, top_ref, from_prev_ref, from_next_ref, weight_ref,
    out_ref, total_ref,
):
    slots, chans = grad_ref.shape
    step = pl.program_id(0)

    @pl.when(step == 0)
    def _():
        total_ref[...] = top_ref[...].astype(jnp.float32)
        total_ref[:F, :] += from_prev_ref[...].astype(jnp.float32)
        total_ref[F : 2 * F, :] += from_next_ref[...].astype(jnp.float32)

    scatter_step(map_ref, weight_ref, grad_ref, total_ref)

    @pl.when(step == pl.num_programs(0) - 1)
    def _():
        live = alive(0, slots, count_ref[0], chans)
        out_ref[...] = (total_ref[...] * live).astype(jnp.bfloat16)


def call(body, name, operands, stepped, outputs, scratch, together=TOGETHER, dense=True):
    offsets = operands[stepped[0]].shape[0]
    unroll = together if offsets % together == 0 else 1
    slots, chans = operands[1].shape[1], operands[stepped[0]].shape[2]
    width = slots if dense else 4 * chans

    def spec(shape, cut):
        if cut:
            return pl.BlockSpec((unroll,) + shape[1:], lambda k: (k,) + (0,) * (len(shape) - 1))
        return pl.BlockSpec(shape, lambda k: (0,) * len(shape))

    specs = [pl.BlockSpec(memory_space=pltpu.SMEM)]
    specs += [spec(o.shape, n in stepped) for n, o in enumerate(operands) if n > 0]
    return pl.pallas_call(
        body,
        grid=(offsets // unroll,),
        in_specs=specs,
        out_specs=[spec(out[0], len(out) > 2) for out in outputs],
        out_shape=[jax.ShapeDtypeStruct(out[0], out[1]) for out in outputs],
        scratch_shapes=[pltpu.VMEM(shape, dtype) for shape, dtype in scratch],
        compiler_params=PARAMS,
        cost_estimate=pl.CostEstimate(
            flops=7 * offsets * slots * width * chans // 2,
            transcendentals=0,
            bytes_accessed=4 * slots * chans,
        ),
        name=name,
    )(*operands)


def swap_rows(rows):
    return lax.all_to_all(rows, AXES, split_axis=0, concat_axis=0, tiled=True)


def local(
    features, kernel_map, send_order, counts, first_weight, second_weight, norm_gain, cotangent
):
    slots, chans = features.shape
    neighbours = kernel_map[0]
    offsets = neighbours.shape[0]
    devices = lax.axis_size(AXES)
    gain = norm_gain[None, :]
    bf16, f32 = jnp.bfloat16, jnp.float32
    rows16, rows32 = ((slots, chans), bf16), ((slots, chans), f32)
    face16 = ((F, chans), bf16)
    table16 = ((TABLE, slots // TABLE * chans), bf16)
    turned16 = ((chans, slots), bf16)

    ends = jnp.arange(2 * F, dtype=jnp.int32)[:, None] < counts[0]
    ends_x = (features[: 2 * F].astype(f32) * ends.astype(f32)).astype(bf16)
    before_x, after_x = shifted(ends_x[F:], 1), shifted(ends_x[:F], -1)
    slotted = swap_rows(cotangent)
    first, hidden, rows_x = call(
        first_layer_body, "first_layer",
        (counts, neighbours, features, before_x, after_x, first_weight, gain), (5,),
        (rows32, rows16, ((offsets, slots, chans), bf16, True)), (table16,),
    )
    edge32 = ((2 * F, chans), f32)
    ends16 = ((2 * F, chans), bf16)
    grad_live, near, upper_up, upper_down = call(
        second_edges_body, "second_edges",
        (counts, neighbours, send_order, slotted, hidden, second_weight), (5,),
        (rows16, ((offsets, 2 * F, chans), bf16, True), ends16, ends16), (edge32,), TOGETHER_EDGES, False,
    )
    below, above = shifted(upper_up, 1), shifted(upper_down, -1)
    upper, partial = call(
        second_back_body, "second_back",
        (counts, neighbours, grad_live, hidden, second_weight), (4,),
        (rows32, ((offsets, chans, chans), f32, True)), (turned16,), TOGETHER_SCATTER,
    )
    grad_first, wgrads, lower_up, lower_down = call(
        weights_body, "weights",
        (counts, neighbours, first, upper, below, above, gain, first_weight, rows_x, near,
         partial), (7, 8, 9, 10),
        (rows16, ((2 * (offsets + 1), chans, chans), bf16), face16, face16),
        (turned16, ((chans, 2 * F), bf16), edge32), TOGETHER_WEIGHTS, False,
    )
    from_prev, from_next = shifted(lower_up, 1), shifted(lower_down, -1)
    parts = swap_rows(wgrads.reshape(devices, -1, chans))
    hidden, grad_first = lax.optimization_barrier((hidden, grad_first))
    (ordered,) = call(
        second_layer_body, "second_layer",
        (counts, neighbours, send_order, features, hidden, below, above, second_weight),
        (7,), (rows16,), (rows32, table16),
    )
    part = jnp.sum(parts.astype(f32), axis=0).astype(bf16)
    ordered, part, grad_first = lax.optimization_barrier((ordered, part, grad_first))
    per_peer = slots // devices
    both = swap_rows(
        jnp.concatenate(
            [
                ordered.reshape(devices, per_peer, chans),
                jnp.broadcast_to(part[None], (devices,) + part.shape),
            ],
            axis=1,
        )
    )
    serial_out = both[:, :per_peer].reshape(slots, chans)
    shared = both[:, per_peer:]
    (grad_features,) = call(
        first_back_body, "first_back",
        (counts, neighbours, grad_first, grad_live, from_prev, from_next, first_weight), (6,),
        (rows16,), (rows32,), TOGETHER_SCATTER,
    )
    shared = shared.reshape(2, offsets + 1, chans, chans)
    first_grad, second_grad = shared[0, :offsets].astype(f32), shared[1, :offsets].astype(f32)
    gain_grad = shared[0, offsets, 0].astype(f32) + shared[0, offsets, 1].astype(f32)
    return (serial_out, grad_features, first_grad, second_grad, gain_grad)


def solution(mesh):
    placed = (
        P(AXES, None),
        P(AXES, None, None),
        P(AXES, None),
        P(AXES),
        P(),
        P(),
        P(),
        P(AXES, None),
    )
    return jax.shard_map(
        local,
        mesh=mesh,
        in_specs=placed,
        out_specs=(P(AXES, None), P(AXES, None), P(), P(), P()),
        check_vma=False,
    )
```

```python
import jax
import jax.numpy as jnp
from jax import lax
from jax.experimental import pallas as pl
from jax.experimental.pallas import tpu as pltpu
from jax.sharding import PartitionSpec as P

F = 256
B = 256
SHIFT = 8
TABLE = 512
TABLE_SHIFT = 9
TOGETHER = 3
TOGETHER_SCATTER = 3
TOGETHER_WEIGHTS = 9
TOGETHER_EDGES = 3
WIDE = 1024
EPS = 1e-05
GELU_SCALE = 0.7978845608028654
GELU_CUBIC = 0.044715
AXES = ("group", "tile")
NT = (((1,), (1,)), ((), ()))
PARAMS = pltpu.CompilerParams(
    dimension_semantics=("arbitrary",), vmem_limit_bytes=58 * 1024 * 1024
)


def shifted(value, steps):
    count = lax.axis_size(AXES)
    initial, last = (max(0, -steps), min(count, count - steps))
    return lax.ppermute(value, AXES, [(source, source + steps) for source in range(initial, last)])


def mm(a, b):
    return jnp.dot(a, b, preferred_element_type=jnp.float32)


def lane_replicated(row):
    parts = [
        jnp.broadcast_to(row[:, j : j + 128], (128, 128)).T for j in range(0, row.shape[1], 128)
    ]
    return jnp.concatenate(parts, axis=0)


def onehot_rows(index, width):
    lanes = lax.broadcasted_iota(jnp.int32, index.shape, 1)
    parts = [
        jnp.where(index == lanes + j, 1.0, 0.0).astype(jnp.bfloat16) for j in range(0, width, 128)
    ]
    return jnp.concatenate(parts, axis=1)


def onehot_cols(row, height):
    shape = (height, row.shape[1])
    return jnp.where(
        jnp.broadcast_to(row, shape) == lax.broadcasted_iota(jnp.int32, shape, 0), 1.0, 0.0
    ).astype(jnp.bfloat16)


def side_mask(entry, side, slots):
    if side == 0:
        return entry < F
    return (entry >= slots + F) & (entry < slots + 2 * F)


def alive(start, size, count, chans):
    rows = lax.broadcasted_iota(jnp.int32, (size, chans), 0) + start
    return jnp.where(rows < count, 1.0, 0.0)


def load_table(table_ref, field, start, size, chans):
    for a in range(start // TABLE, (start + size) // TABLE):
        at = a * TABLE - start
        table_ref[:, a * chans : (a + 1) * chans] = field[at : at + TABLE]


def pick(index, table_ref, chans):
    picked = mm(onehot_rows(index & (TABLE - 1), TABLE), table_ref[...])
    high = index >> TABLE_SHIFT
    rows = jnp.where(high == 0, picked[:, :chans], 0.0)
    for a in range(1, table_ref.shape[1] // chans):
        rows = jnp.where(high == a, picked[:, a * chans : (a + 1) * chans], rows)
    return rows


def drop(row, index, value, groups):
    high = index >> SHIFT
    spread = jnp.concatenate(
        [jnp.where(high == a, value, 0.0).astype(jnp.bfloat16) for a in range(groups)], axis=1
    )
    return mm(onehot_cols(row & (B - 1), B), spread)


def normalise(first, gain):
    centred = first - jnp.mean(first, axis=-1, keepdims=True)
    inv_std = lax.rsqrt(jnp.mean(centred * centred, axis=-1, keepdims=True) + EPS)
    unit = centred * inv_std
    normed = unit * gain
    bent = jnp.tanh(GELU_SCALE * (normed + GELU_CUBIC * (normed * normed * normed)))
    return unit, inv_std, normed, bent


def gather_step(
    map_ref, before_ref, after_ref, weight_ref, out_ref, table_ref, slots, chans, keep_ref=None
):
    step = pl.program_id(0)
    unroll = weight_ref.shape[0]
    weight = weight_ref[...].reshape(unroll * chans, chans)
    for start in range(0, slots, WIDE):
        size = min(WIDE, slots - start)
        found = []
        for u in range(unroll):
            entry = lane_replicated(map_ref[pl.ds(step * unroll + u, 1), start : start + size])
            rows = pick(entry - F, table_ref, chans)
            parts = []
            for side, face_ref in enumerate((before_ref, after_ref)):
                at = side * F - start
                if 0 <= at < size:
                    near = entry[at : at + F]
                    crossing = mm(onehot_rows(near & (F - 1), F), face_ref[...])
                    parts.append(
                        jnp.where(side_mask(near, side, slots), crossing, rows[at : at + F])
                    )
            if parts:
                parts.append(rows[len(parts) * F :])
                rows = jnp.concatenate(parts, axis=0)
            found.append(rows.astype(jnp.bfloat16))
            if keep_ref is not None:
                keep_ref[u, start : start + size, :] = found[-1]
        out_ref[start : start + size, :] += mm(jnp.concatenate(found, axis=1), weight)


def first_layer_body(
    count_ref, map_ref, field_ref, before_ref, after_ref, weight_ref, gain_ref,
    first_ref, hidden_ref, rows_ref, table_ref,
):
    slots, chans = field_ref.shape
    step = pl.program_id(0)

    @pl.when(step == 0)
    def _():
        first_ref[...] = jnp.zeros_like(first_ref)
        for start in range(0, slots, TABLE):
            field = field_ref[start : start + TABLE, :].astype(jnp.float32)
            field = (field * alive(start, TABLE, count_ref[0], chans)).astype(jnp.bfloat16)
            load_table(table_ref, field, start, TABLE, chans)

    gather_step(
        map_ref, before_ref, after_ref, weight_ref, first_ref, table_ref, slots, chans, rows_ref
    )

    @pl.when(step == pl.num_programs(0) - 1)
    def _():
        for start in range(0, slots, B):
            at = slice(start, start + B)
            _, _, normed, bent = normalise(first_ref[at, :], gain_ref[...])
            act = 0.5 * normed * (1.0 + bent)
            hidden_ref[at, :] = (act * alive(start, B, count_ref[0], chans)).astype(jnp.bfloat16)


def second_layer_body(
    count_ref, map_ref, order_ref, skip_ref, field_ref, below_ref, above_ref, weight_ref,
    serial_ref, second_ref, table_ref,
):
    slots, chans = field_ref.shape
    step = pl.program_id(0)

    @pl.when(step == 0)
    def _():
        second_ref[...] = jnp.zeros_like(second_ref)
        load_table(table_ref, field_ref, 0, slots, chans)

    faces = (below_ref.at[pl.ds(F, F), :], above_ref.at[pl.ds(F, F), :])
    gather_step(map_ref, *faces, weight_ref, second_ref, table_ref, slots, chans)

    @pl.when(step == pl.num_programs(0) - 1)
    def _():
        for start in range(0, slots, TABLE):
            at = slice(start, start + TABLE)
            live = alive(start, TABLE, count_ref[0], chans)
            masked = skip_ref[at, :].astype(jnp.float32) * live
            block = ((masked + second_ref[at, :]) * live).astype(jnp.bfloat16)
            load_table(table_ref, block, start, TABLE, chans)
        for start in range(0, slots, WIDE):
            size = min(WIDE, slots - start)
            index = lane_replicated(order_ref[:, start : start + size])
            serial_ref[start : start + size, :] = pick(index, table_ref, chans).astype(
                jnp.bfloat16
            )


def edge_step(map_ref, weight_ref, grad_ref, edge_ref, near_ref=None):
    chans = grad_ref.shape[1]
    slots = grad_ref.shape[0]
    step = pl.program_id(0)
    unroll = weight_ref.shape[0]
    back = jnp.concatenate([weight_ref[u] for u in range(unroll)], axis=1)
    for side in range(2):
        at = slice(side * F, (side + 1) * F)
        grad = grad_ref[at, :].astype(jnp.float32)
        sums = []
        for u in range(unroll):
            row = map_ref[pl.ds(step * unroll + u, 1), at]
            crossing = jnp.where(side_mask(lane_replicated(row), side, slots), grad, 0.0)
            sums.append(
                mm(onehot_cols(row & (F - 1), F), crossing.astype(jnp.bfloat16)).astype(
                    jnp.bfloat16
                )
            )
            if near_ref is not None:
                near_ref[u, at, :] = sums[-1]
        edge_ref[at, :] += lax.dot_general(
            jnp.concatenate(sums, axis=1), back, NT, preferred_element_type=jnp.float32
        )


def scatter_step(map_ref, weight_ref, grad_ref, total_ref, turned_ref=None, wgrad_ref=None):
    slots, chans = grad_ref.shape
    groups = slots // B
    step = pl.program_id(0)
    unroll = weight_ref.shape[0]
    own = []
    for u in range(unroll):
        row = map_ref[pl.ds(step * unroll + u, 1), :]
        grad = grad_ref[...].astype(jnp.float32)
        own.append(drop(row - F, lane_replicated(row) - F, grad, groups).astype(jnp.bfloat16))
    back = jnp.concatenate([weight_ref[u] for u in range(unroll)], axis=1)
    wide = None
    for a in range(groups):
        piece = jnp.concatenate(
            [own[u][:, a * chans : (a + 1) * chans] for u in range(unroll)], axis=1
        )
        at = slice(a * B, (a + 1) * B)
        total_ref[at, :] += lax.dot_general(piece, back, NT, preferred_element_type=jnp.float32)
        if wgrad_ref is not None:
            term = mm(turned_ref[:, at], piece)
            wide = term if wide is None else wide + term
    if wgrad_ref is not None:
        for u in range(unroll):
            wgrad_ref[u] = wide[:, u * chans : (u + 1) * chans]


def second_edges_body(
    count_ref, map_ref, order_ref, slotted_ref, ends_ref, weight_ref,
    grad_ref, near_ref, up_ref, down_ref, edge_ref,
):
    slots, chans = slotted_ref.shape
    step = pl.program_id(0)

    @pl.when(step == 0)
    def _():
        edge_ref[...] = jnp.zeros_like(edge_ref)
        order = order_ref[...]
        placed = drop(
            order, lane_replicated(order), slotted_ref[...].astype(jnp.float32), slots // B
        )
        for a in range(slots // B):
            live = alive(a * B, B, count_ref[0], chans)
            grad_ref[a * B : (a + 1) * B, :] = (
                placed[:, a * chans : (a + 1) * chans] * live
            ).astype(jnp.bfloat16)

    edge_step(map_ref, weight_ref, grad_ref, edge_ref, near_ref)

    @pl.when(step == pl.num_programs(0) - 1)
    def _():
        up_ref[:F, :] = edge_ref[F:, :].astype(jnp.bfloat16)
        up_ref[F:, :] = ends_ref[F : 2 * F, :]
        down_ref[:F, :] = edge_ref[:F, :].astype(jnp.bfloat16)
        down_ref[F:, :] = ends_ref[:F, :]


def second_back_body(
    count_ref, map_ref, grad_ref, field_ref, weight_ref, total_ref, wgrad_ref, turned_ref
):
    step = pl.program_id(0)

    @pl.when(step == 0)
    def _():
        total_ref[...] = jnp.zeros_like(total_ref)
        turned_ref[...] = field_ref[...].T

    scatter_step(map_ref, weight_ref, grad_ref, total_ref, turned_ref, wgrad_ref)


def weights_body(
    count_ref, map_ref, first_ref, upper_ref, below_ref, above_ref, gain_ref,
    weight_ref, rows_ref, near_ref, partial_ref,
    grad_ref, wgrad_ref, up_ref, down_ref, turned_ref, faces_ref, edge_ref,
):
    slots, chans = first_ref.shape
    step = pl.program_id(0)
    unroll = rows_ref.shape[0]
    half = wgrad_ref.shape[0] // 2

    @pl.when(step == 0)
    def _():
        edge_ref[...] = jnp.zeros_like(edge_ref)
        gain_term = jnp.zeros((1, chans), jnp.float32)
        faces_ref[:, :F] = below_ref[F:, :].T
        faces_ref[:, F:] = above_ref[F:, :].T
        for start in range(0, slots, B):
            at = slice(start, start + B)
            live = alive(start, B, count_ref[0], chans)
            upper = upper_ref[at, :]
            if start == 0:
                upper = upper + below_ref[:F, :].astype(jnp.float32)
            if start == F:
                upper = upper + above_ref[:F, :].astype(jnp.float32)
            unit, inv_std, normed, bent = normalise(first_ref[at, :], gain_ref[...])
            inner = GELU_SCALE * (1.0 + 3.0 * GELU_CUBIC * (normed * normed))
            slope = 0.5 * (1.0 + bent) + 0.5 * normed * (1.0 - bent * bent) * inner
            grad_normed = slope * (upper * live)
            gain_term = gain_term + jnp.sum(grad_normed * unit, axis=0, keepdims=True)
            grad_unit = grad_normed * gain_ref[...]
            centred = (
                grad_unit
                - jnp.mean(grad_unit, axis=-1, keepdims=True)
                - unit * jnp.mean(grad_unit * unit, axis=-1, keepdims=True)
            )
            grad = (inv_std * centred).astype(jnp.bfloat16)
            grad_ref[at, :] = grad
            turned_ref[:, at] = grad.T
        row = lax.broadcasted_iota(jnp.int32, (chans, chans), 0)
        high = gain_term.astype(jnp.bfloat16).astype(jnp.float32)
        wgrad_ref[half - 1] = jnp.where(
            row == 0, high, jnp.where(row == 1, gain_term - high, 0.0)
        ).astype(jnp.bfloat16)
        wgrad_ref[2 * half - 1] = jnp.zeros((chans, chans), jnp.bfloat16)

    edge_step(map_ref, weight_ref, grad_ref, edge_ref)
    wide = mm(turned_ref[...], jnp.concatenate([rows_ref[u] for u in range(unroll)], axis=1))
    edge = mm(faces_ref[...], jnp.concatenate([near_ref[u] for u in range(unroll)], axis=1))
    for u in range(unroll):
        at = slice(u * chans, (u + 1) * chans)
        wgrad_ref[step * unroll + u] = wide[:, at].T.astype(jnp.bfloat16)
        wgrad_ref[half + step * unroll + u] = (partial_ref[u] + edge[:, at]).astype(jnp.bfloat16)

    @pl.when(step == pl.num_programs(0) - 1)
    def _():
        up_ref[...] = edge_ref[F:, :].astype(jnp.bfloat16)
        down_ref[...] = edge_ref[:F, :].astype(jnp.bfloat16)


def first_back_body(
    count_ref, map_ref, grad_ref, top_ref, from_prev_ref, from_next_ref, weight_ref,
    out_ref, total_ref,
):
    slots, chans = grad_ref.shape
    step = pl.program_id(0)

    @pl.when(step == 0)
    def _():
        total_ref[...] = top_ref[...].astype(jnp.float32)
        total_ref[:F, :] += from_prev_ref[...].astype(jnp.float32)
        total_ref[F : 2 * F, :] += from_next_ref[...].astype(jnp.float32)

    scatter_step(map_ref, weight_ref, grad_ref, total_ref)

    @pl.when(step == pl.num_programs(0) - 1)
    def _():
        live = alive(0, slots, count_ref[0], chans)
        out_ref[...] = (total_ref[...] * live).astype(jnp.bfloat16)


def call(body, name, operands, stepped, outputs, scratch, together=TOGETHER, dense=True):
    offsets = operands[stepped[0]].shape[0]
    unroll = together if offsets % together == 0 else 1
    slots, chans = operands[1].shape[1], operands[stepped[0]].shape[2]
    width = slots if dense else 4 * chans

    def spec(shape, cut):
        if cut:
            return pl.BlockSpec((unroll,) + shape[1:], lambda k: (k,) + (0,) * (len(shape) - 1))
        return pl.BlockSpec(shape, lambda k: (0,) * len(shape))

    specs = [pl.BlockSpec(memory_space=pltpu.SMEM)]
    specs += [spec(o.shape, n in stepped) for n, o in enumerate(operands) if n > 0]
    return pl.pallas_call(
        body,
        grid=(offsets // unroll,),
        in_specs=specs,
        out_specs=[spec(out[0], len(out) > 2) for out in outputs],
        out_shape=[jax.ShapeDtypeStruct(out[0], out[1]) for out in outputs],
        scratch_shapes=[pltpu.VMEM(shape, dtype) for shape, dtype in scratch],
        compiler_params=PARAMS,
        cost_estimate=pl.CostEstimate(
            flops=7 * offsets * slots * width * chans // 2,
            transcendentals=0,
            bytes_accessed=4 * slots * chans,
        ),
        name=name,
    )(*operands)


def swap_rows(rows):
    return lax.all_to_all(rows, AXES, split_axis=0, concat_axis=0, tiled=True)


def local(
    features, kernel_map, send_order, counts, first_weight, second_weight, norm_gain, cotangent
):
    slots, chans = features.shape
    neighbours = kernel_map[0]
    offsets = neighbours.shape[0]
    devices = lax.axis_size(AXES)
    gain = norm_gain[None, :]
    bf16, f32 = jnp.bfloat16, jnp.float32
    rows16, rows32 = ((slots, chans), bf16), ((slots, chans), f32)
    face16 = ((F, chans), bf16)
    table16 = ((TABLE, slots // TABLE * chans), bf16)
    turned16 = ((chans, slots), bf16)

    ends = jnp.arange(2 * F, dtype=jnp.int32)[:, None] < counts[0]
    ends_x = (features[: 2 * F].astype(f32) * ends.astype(f32)).astype(bf16)
    before_x, after_x = shifted(ends_x[F:], 1), shifted(ends_x[:F], -1)
    slotted = swap_rows(cotangent)
    first, hidden, rows_x = call(
        first_layer_body, "first_layer",
        (counts, neighbours, features, before_x, after_x, first_weight, gain), (5,),
        (rows32, rows16, ((offsets, slots, chans), bf16, True)), (table16,),
    )
    edge32 = ((2 * F, chans), f32)
    ends16 = ((2 * F, chans), bf16)
    grad_live, near, upper_up, upper_down = call(
        second_edges_body, "second_edges",
        (counts, neighbours, send_order, slotted, hidden, second_weight), (5,),
        (rows16, ((offsets, 2 * F, chans), bf16, True), ends16, ends16), (edge32,), TOGETHER_EDGES, False,
    )
    below, above = shifted(upper_up, 1), shifted(upper_down, -1)
    upper, partial = call(
        second_back_body, "second_back",
        (counts, neighbours, grad_live, hidden, second_weight), (4,),
        (rows32, ((offsets, chans, chans), f32, True)), (turned16,), TOGETHER_SCATTER,
    )
    grad_first, wgrads, lower_up, lower_down = call(
        weights_body, "weights",
        (counts, neighbours, first, upper, below, above, gain, first_weight, rows_x, near,
         partial), (7, 8, 9, 10),
        (rows16, ((2 * (offsets + 1), chans, chans), bf16), face16, face16),
        (turned16, ((chans, 2 * F), bf16), edge32), TOGETHER_WEIGHTS, False,
    )
    from_prev, from_next = shifted(lower_up, 1), shifted(lower_down, -1)
    parts = swap_rows(wgrads.reshape(devices, -1, chans))
    hidden, grad_first = lax.optimization_barrier((hidden, grad_first))
    (ordered,) = call(
        second_layer_body, "second_layer",
        (counts, neighbours, send_order, features, hidden, below, above, second_weight),
        (7,), (rows16,), (rows32, table16),
    )
    part = jnp.sum(parts.astype(f32), axis=0).astype(bf16)
    ordered, part, grad_first = lax.optimization_barrier((ordered, part, grad_first))
    per_peer = slots // devices
    both = swap_rows(
        jnp.concatenate(
            [
                ordered.reshape(devices, per_peer, chans),
                jnp.broadcast_to(part[None], (devices,) + part.shape),
            ],
            axis=1,
        )
    )
    serial_out = both[:, :per_peer].reshape(slots, chans)
    shared = both[:, per_peer:]
    (grad_features,) = call(
        first_back_body, "first_back",
        (counts, neighbours, grad_first, grad_live, from_prev, from_next, first_weight), (6,),
        (rows16,), (rows32,), TOGETHER_SCATTER,
    )
    shared = shared.reshape(2, offsets + 1, chans, chans)
    first_grad, second_grad = shared[0, :offsets].astype(f32), shared[1, :offsets].astype(f32)
    gain_grad = shared[0, offsets, 0].astype(f32) + shared[0, offsets, 1].astype(f32)
    return (serial_out, grad_features, first_grad, second_grad, gain_grad)


def solution(mesh):
    placed = (
        P(AXES, None),
        P(AXES, None, None),
        P(AXES, None),
        P(AXES),
        P(),
        P(),
        P(),
        P(AXES, None),
    )
    return jax.shard_map(
        local,
        mesh=mesh,
        in_specs=placed,
        out_specs=(P(AXES, None), P(AXES, None), P(), P(), P()),
        check_vma=False,
    )
```
